256 devices in a mesh: dp: 16 (over y, x), expert: 16 (over z, core).
Axes of the slice: x: 4, y: 4, z: 8, core: 2. Of those that a mesh axis runs over, the one named last changes fastest.
Arguments:
- tokens: bfloat16 [32768, 2048], P(('dp', 'expert')), may hold values from -6 to 6
- initial_expert_index: int32 [32768, 4], P(('dp', 'expert')), may hold values from 0 to 31, all different within a row; in each aligned block of 128 rows (0 to 127, 128 to 255, ...) at most 18 rows name the same one
- pruned_expert_index: int32 [32768, 4], P(('dp', 'expert')), may hold values from 0 to 15, all different within a row; in each aligned block of 128 rows (0 to 127, 128 to 255, ...) at most 36 rows name the same one
- initial_router_scores: float32 [32768, 4], P(('dp', 'expert')), may hold values from 0.05 to 1
- pruned_router_scores: float32 [32768, 4], P(('dp', 'expert')), may hold values from 0.05 to 1
- gate_weight: bfloat16 [32, 2048, 768], P('expert', 'dp'), may hold values from -0.125 to 0.125
- up_weight: bfloat16 [32, 2048, 768], P('expert', 'dp'), may hold values from -0.125 to 0.125
- down_weight: bfloat16 [32, 768, 2048], P('expert', None, 'dp'), may hold values from -0.21875 to 0.21875
- adapter_first_weight: float32 [16, 768, 64], P('expert'), may hold values from -0.21875 to 0.21875
- adapter_second_weight: float32 [16, 64, 2048], P('expert'), may hold values from -0.75 to 0.75
Outputs:
- grad_a: float32 [16, 768, 64], P('expert', 'dp')
- grad_b: float32 [16, 64, 2048], P('expert', None, 'dp')
The draws below stay inside these ranges and needn't reach their ends.
Inputs may be any that keep to these rules, and one draw needn't show every extreme that they name: `initial_expert_index`: the 4 entries of a row differ. In each aligned block of 128 rows no expert is named more than 18 times, a bound that some block reaches. `pruned_expert_index`: the 4 entries of a row differ. In each aligned block of 128 rows no expert is named more than 36 times, a bound that some block reaches.
All inputs are finite; a program needn't handle non-finite values.
Results may differ from the reference program's by a relative error of at most 0.0029.
Values may be sent and summed in bfloat16 or wider, within the bound.
A program may use at most 128 MiB of HBM per device.

```python
import math
import jax
import jax.numpy as jnp
import numpy as np
from jax import lax

MODEL_WIDTH = 2048
EXPERT_HIDDEN = 768
ADAPTER_RANK = 64
TOPK = 4
TOK_DEV = 128
TOKENS = 32768
EXPERTS = 32
PRUNED_EXPERTS = 16
CAP_O = 18
CAP_P = 36


def level_of(key, dims, cuts, least, largest):
    def one(dim, shards_of):
        draws = jax.random.uniform(jax.random.fold_in(jax.random.fold_in(key, 6), dim), (shards_of,), jnp.float32, least / len(cuts), largest / len(cuts))
        return jnp.repeat(jnp.exp(draws), dims[dim] // shards_of).reshape((-1,) + (1,) * (len(dims) - dim - 1))

    level = one(*cuts[0])
    for cut in cuts[1:]:
        level = level * one(*cut)
    return level


def assign_block(key, own, number, rows, count, top, reach, skew):
    sequence = jax.random.permutation(key, count)
    heavy_load, common = load_shares(count, rows * top, reach, skew, True), load_shares(count, rows * top, reach, skew, False)
    places = jnp.arange(count)

    def named(tallies, turn):
        used = int((tallies > 0).sum())
        fixed = max(1, used // 4)
        moved = fixed + (places - fixed + turn * (used - fixed)) % max(1, count - fixed)
        return jnp.zeros((count,), jnp.int32).at[sequence[jnp.where(places < fixed, places, moved)]].set(jnp.asarray(tallies, jnp.int32))

    tallies = jnp.where(number % 4 == 0, named(heavy_load, number // 4), named(common, number - number // 4 - 1))
    mixed = jax.random.permutation(jax.random.fold_in(own, 3), count)
    source_of, receiver = mixed[0:count // 2 * 2:2], mixed[1:count // 2 * 2:2]
    slack = jnp.minimum(tallies[source_of] - 1, reach - tallies[receiver]) // 2
    slack = jnp.where((source_of == sequence[0]) | (receiver == sequence[0]) | (tallies[receiver] == 0), 0, jnp.maximum(slack, 0))
    moved = jax.random.randint(jax.random.fold_in(own, 4), (count // 2,), 0, 1 << 20) % (slack + 1)
    tallies = tallies.at[source_of].add(-moved).at[receiver].add(moved)
    members = jnp.searchsorted(jnp.cumsum(tallies), jnp.arange(rows * top), side="right").astype(jnp.int32)
    table = members.reshape(top, rows).T
    table = table[jax.random.permutation(jax.random.fold_in(own, 1), rows)]
    turn = jax.random.randint(jax.random.fold_in(own, 2), (rows, 1), 0, top)
    return jnp.take_along_axis(table, (jnp.arange(top)[None, :] + turn) % top, axis=1)


def load_shares(number_of, total, limit, slope, full):
    portions = [(1 << 20) // math.isqrt(standing ** slope) + 1 for standing in range(1, number_of + 1)]
    largest = limit if full else min(limit, max(-(-total // number_of), total * portions[0] // sum(portions)))
    least = 1 if total - largest >= number_of - 1 else 0
    holding, rest = [largest] + [least] * (number_of - 1), total - largest - least * (number_of - 1)
    while rest > 0:
        candidates = [i for i in range(1, number_of) if holding[i] < largest] or [i for i in range(1, number_of) if holding[i] < limit]
        mass, budget = sum([portions[i] for i in candidates]), rest
        for i in candidates:
            extra = min(limit - holding[i], max(1, budget * portions[i] // mass), rest)
            holding[i] = holding[i] + extra
            rest = rest - extra
    return np.array(holding)


def normal_values(stream_key, dims, width, most, pieces=(), held_as=jnp.bfloat16):
    array = jax.random.normal(stream_key, dims, jnp.float32) * width
    if len(pieces) > 0:
        array = level_of(stream_key, dims, pieces, -0.22, 0.18) * array
    return jnp.clip(array, min=-most, max=most).astype(held_as)


def setup_inputs(seed: int = 0) -> dict:
    splits = jax.random.split(jax.random.key(seed), 11)
    tokens = normal_values(splits[0], (TOKENS, MODEL_WIDTH), 1.0, 6.0, ((0, 256),))
    initial_expert_index_keys = jax.random.split(jax.random.fold_in(splits[1], 1), TOKENS // TOK_DEV)
    initial_expert_index_turns = jax.random.permutation(jax.random.fold_in(splits[1], 3), TOKENS // TOK_DEV)
    initial_expert_index = jax.vmap(lambda own, number: assign_block(jax.random.fold_in(splits[1], 2), own, number, TOK_DEV, EXPERTS, TOPK, CAP_O, 1))(initial_expert_index_keys, initial_expert_index_turns).reshape((TOKENS, TOPK))
    pruned_expert_index_keys = jax.random.split(jax.random.fold_in(splits[2], 1), TOKENS // TOK_DEV)
    pruned_expert_index_turns = jax.random.permutation(jax.random.fold_in(splits[2], 3), TOKENS // TOK_DEV)
    pruned_expert_index = jax.vmap(lambda own, number: assign_block(jax.random.fold_in(splits[2], 2), own, number, TOK_DEV, PRUNED_EXPERTS, TOPK, CAP_P, 1))(pruned_expert_index_keys, pruned_expert_index_turns).reshape((TOKENS, TOPK))
    initial_router_scores = jnp.clip(0.05 + 0.95 * jax.random.uniform(splits[3], (TOKENS, TOPK), jnp.float32) ** level_of(splits[3], (TOKENS, TOPK), ((0, 256),), -0.2, 0.2), 0.05, 1.0)
    pruned_router_scores = jnp.clip(0.05 + 0.95 * jax.random.uniform(splits[4], (TOKENS, TOPK), jnp.float32) ** level_of(splits[4], (TOKENS, TOPK), ((0, 256),), -0.2, 0.2), 0.05, 1.0)
    gate_weight = normal_values(splits[5], (EXPERTS, MODEL_WIDTH, EXPERT_HIDDEN), MODEL_WIDTH ** -0.5, 0.125, ((0, 16), (1, 16)))
    up_weight = normal_values(splits[6], (EXPERTS, MODEL_WIDTH, EXPERT_HIDDEN), MODEL_WIDTH ** -0.5, 0.125, ((0, 16), (1, 16)))
    down_weight = normal_values(splits[7], (EXPERTS, EXPERT_HIDDEN, MODEL_WIDTH), EXPERT_HIDDEN ** -0.5, 0.21875, ((0, 16), (2, 16)))
    adapter_first_weight = normal_values(splits[8], (PRUNED_EXPERTS, EXPERT_HIDDEN, ADAPTER_RANK), EXPERT_HIDDEN ** -0.5, 0.21875, ((0, 16),), jnp.float32)
    adapter_second_weight = normal_values(splits[9], (PRUNED_EXPERTS, ADAPTER_RANK, MODEL_WIDTH), ADAPTER_RANK ** -0.5, 0.75, ((0, 16),), jnp.float32)
    return dict(tokens=tokens, initial_expert_index=initial_expert_index, pruned_expert_index=pruned_expert_index, initial_router_scores=initial_router_scores, pruned_router_scores=pruned_router_scores, gate_weight=gate_weight, up_weight=up_weight, down_weight=down_weight, adapter_first_weight=adapter_first_weight, adapter_second_weight=adapter_second_weight)


def route_tables(route_ids, weight, num_experts, capacity):
    blocks = route_ids.shape[0] // TOK_DEV
    shares = weight / jnp.sum(weight, axis=1, keepdims=True)
    flat_ids = route_ids.reshape(blocks, TOK_DEV * TOPK)
    hit_table = (flat_ids[:, :, None] == jnp.arange(num_experts, dtype=jnp.int32)[None, None, :]).astype(jnp.int32)
    slot_index = jnp.sum(hit_table * (jnp.cumsum(hit_table, axis=1) - 1), axis=2)
    block_base = (jnp.arange(blocks, dtype=jnp.int32) * (num_experts * capacity))[:, None]
    dest_index = (block_base + flat_ids * capacity + slot_index).reshape(-1)
    owner_token = ((jnp.arange(blocks, dtype=jnp.int32) * TOK_DEV)[:, None] + jnp.arange(TOK_DEV * TOPK, dtype=jnp.int32)[None, :] // TOPK).reshape(-1)
    slot_token = jnp.zeros(blocks * num_experts * capacity, jnp.int32).at[dest_index].set(owner_token)
    slot_weight = jnp.zeros(blocks * num_experts * capacity, jnp.float32).at[dest_index].set(shares.reshape(-1))
    slot_token = slot_token.reshape(blocks, num_experts, capacity).transpose(1, 0, 2).reshape(num_experts, -1)
    slot_weight = slot_weight.reshape(blocks, num_experts, capacity).transpose(1, 0, 2).reshape(num_experts, -1)
    return slot_token, slot_weight


def hidden_rows(rows, gate_mat, up_mat):
    gate_part = jnp.dot(rows, gate_mat, preferred_element_type=jnp.float32)
    up_part = jnp.dot(rows, up_mat, preferred_element_type=jnp.float32)
    return (jax.nn.silu(gate_part) * up_part).astype(jnp.bfloat16)


def reference(tokens, initial_expert_index, pruned_expert_index, initial_router_scores, pruned_router_scores, gate_weight, up_weight, down_weight, adapter_first_weight, adapter_second_weight):
    frozen_tok, frozen_wts = route_tables(initial_expert_index, initial_router_scores, EXPERTS, CAP_O)
    pruned_token_rows, pruned_gate_weights = route_tables(pruned_expert_index, pruned_router_scores, PRUNED_EXPERTS, CAP_P)
    offset_index = jnp.zeros(tokens.shape, jnp.float32)

    def frozen_step(total, inputs):
        tok_index, tok_share, gate_mat, up_mat, down_mat = inputs
        rows = jnp.take(tokens, tok_index, axis=0)
        hidden = hidden_rows(rows, gate_mat, up_mat)
        frozen_row = jnp.dot(hidden, down_mat, preferred_element_type=jnp.float32).astype(jnp.bfloat16)
        return total.at[tok_index].add(frozen_row.astype(jnp.float32) * tok_share[:, None]), None

    target, discarded_value = lax.scan(frozen_step, offset_index, (frozen_tok, frozen_wts, gate_weight, up_weight, down_weight))

    def pruned_update(total, inputs):
        tok_index, tok_share, gate_mat, up_mat, down_mat, first_factor, second_factor = inputs
        rows = jnp.take(tokens, tok_index, axis=0)
        hidden = hidden_rows(rows, gate_mat, up_mat)
        hidden_full_width = lax.optimization_barrier(hidden).astype(jnp.float32)
        lowrank_hidden = jnp.dot(hidden_full_width, first_factor, precision=lax.Precision.HIGHEST)
        base = jnp.dot(hidden, down_mat, preferred_element_type=jnp.float32)
        pruned_row = (base + jnp.dot(lowrank_hidden, second_factor, precision=lax.Precision.HIGHEST)).astype(jnp.bfloat16)
        total = total.at[tok_index].add(pruned_row.astype(jnp.float32) * tok_share[:, None])
        return total, (hidden, lowrank_hidden)

    pruned_estimate, stored_residuals = lax.scan(pruned_update, offset_index, (pruned_token_rows, pruned_gate_weights, gate_weight[0::2], up_weight[0::2], down_weight[0::2], adapter_first_weight, adapter_second_weight))
    residual = pruned_estimate - target

    def gradient_update(carry, inputs):
        tok_index, tok_share, hidden, lowrank_hidden, second_factor = inputs
        grad_row = (jnp.take(residual, tok_index, axis=0) * tok_share[:, None]).astype(jnp.bfloat16)
        gradient_hidden_full = lax.optimization_barrier(grad_row).astype(jnp.float32)
        part_b = jnp.dot(lowrank_hidden.T, gradient_hidden_full, precision=lax.Precision.HIGHEST)
        backward_lowrank = jnp.dot(gradient_hidden_full, second_factor.T, precision=lax.Precision.HIGHEST)
        hidden_full_width = lax.optimization_barrier(hidden).astype(jnp.float32)
        part_a = jnp.dot(hidden_full_width.T, backward_lowrank, precision=lax.Precision.HIGHEST)
        return carry, (part_a, part_b)

    discarded_value, adapter_gradients = lax.scan(gradient_update, jnp.zeros((), jnp.float32), (pruned_token_rows, pruned_gate_weights, stored_residuals[0], stored_residuals[1], adapter_second_weight))
    return adapter_gradients[0], adapter_gradients[1]
```

```python
import functools

import jax
import jax.numpy as jnp
from jax import lax
from jax.experimental import pallas as pl
from jax.experimental.pallas import tpu as pltpu
from jax.sharding import PartitionSpec as P

BF = jnp.bfloat16
F32 = jnp.float32
MESH = pl.DeviceIdType.MESH
ANY = pl.BlockSpec(memory_space=pl.ANY)
VM = pl.BlockSpec(memory_space=pltpu.VMEM)

NX = 4
NZ = 8
GROUP = 16
BLOCK = 128
WIDTH = 2048
HIDDEN = 768
RANK = 64
QUADS = 4
TOKQ = 4 * BLOCK
CAPF = 18
CAPP = 36
RF = 80
RP = 144
RQ = 2 * RF + RP
ROWS0 = QUADS * (RF + RP)
ROWS1 = QUADS * RF
CHUNK = 256


class Place:
    def __init__(self):
        dp, ex = lax.axis_index("dp"), lax.axis_index("expert")
        self.dp, self.ex = dp, ex
        self.x, self.y = lax.rem(dp, NX), lax.div(dp, NX)
        self.z, self.c = lax.div(ex, 2), lax.rem(ex, 2)

    def xy(self, dx, dy):
        return lax.rem(self.y + dy + NX, NX) * NX + lax.rem(self.x + dx + NX, NX)

    def zz(self, dz):
        return lax.rem(self.z + dz + NZ, NZ)

    def dev_xy(self, dx, dy):
        return (self.xy(dx, dy), self.ex)

    def dev_z(self, dz):
        return (self.dp, self.zz(dz) * 2 + self.c)

    def partner(self):
        return (self.dp, self.z * 2 + 1 - self.c)


def barrier(devices):
    sem = pltpu.get_barrier_semaphore()
    for d in devices:
        pl.semaphore_signal(sem, inc=1, device_id=d, device_id_type=MESH)
    pl.semaphore_wait(sem, len(devices))


class Sender:
    def __init__(self, send_sem, recv_sem):
        self.send_sem, self.recv_sem = send_sem, recv_sem
        self.count = 0
        self.sent = []

    def send(self, src, dst, device):
        n = self.count
        self.count += 1
        cp = pltpu.make_async_remote_copy(
            src_ref=src, dst_ref=dst, send_sem=self.send_sem.at[n], recv_sem=self.recv_sem.at[n],
            device_id=device, device_id_type=MESH,
        )
        cp.start()
        self.sent.append(cp)
        return n

    def arrived(self, n, region, device):
        pltpu.make_async_remote_copy(
            src_ref=region, dst_ref=region, send_sem=self.send_sem.at[n], recv_sem=self.recv_sem.at[n],
            device_id=device, device_id_type=MESH,
        ).wait_recv()

    def finish(self):
        for cp in self.sent:
            cp.wait_send()


def gather_z(me, tx, own, region):
    c = me.c
    half = own.shape[0] // 2

    def part(ref, h):
        return ref if h is None else ref.at[pl.ds(h * half, half)]

    plus = tx.send(own, region(me.z, c, None), me.dev_z(1))
    minus = tx.send(own, region(me.z, c, None), me.dev_z(-1))
    got = [(tx.send(own, region(me.z, c, None), me.partner()), 0, None)]
    yield
    for k in (1, 2, 3):
        zl, zr = me.zz(-k), me.zz(k)
        tx.arrived(plus, region(zl, c, None), me.dev_z(1))
        plus = (tx.send(region(zl, c, None), region(zl, c, None), me.dev_z(1)) if k < 3
                else tx.send(region(zl, c, 0), region(zl, c, 0), me.dev_z(1)))
        got.append((tx.send(region(zl, c, None), region(zl, c, None), me.partner()), -k, None))
        tx.arrived(minus, region(zr, c, None), me.dev_z(-1))
        minus = (tx.send(region(zr, c, None), region(zr, c, None), me.dev_z(-1)) if k < 3
                 else tx.send(region(zr, c, 1), region(zr, c, 1), me.dev_z(-1)))
        got.append((tx.send(region(zr, c, None), region(zr, c, None), me.partner()), k, None))
        yield
    zo = me.zz(4)
    tx.arrived(plus, region(zo, c, 0), me.dev_z(1))
    got.append((tx.send(region(zo, c, 0), region(zo, c, 0), me.partner()), 4, 0))
    tx.arrived(minus, region(zo, c, 1), me.dev_z(-1))
    got.append((tx.send(region(zo, c, 1), region(zo, c, 1), me.partner()), 4, 1))
    yield
    for n, k, h in got:
        tx.arrived(n, region(me.zz(k), 1 - c, h), me.partner())
    yield


def gather_xy(me, tx, own, region, x_first):
    def at(p, q):
        return (p, q) if x_first else (q, p)

    def idx(p, q):
        return me.xy(*at(p, q))

    def dev(p, q):
        return me.dev_xy(*at(p, q))

    def src(p, q, h):
        return own(h) if (p, q) == (0, 0) else region(idx(p, q), h)

    def ring(p, q, along):
        dp_, dq_ = (1, 0) if along == "p" else (0, 1)
        a = tx.send(src(p, q, None), region(idx(p, q), None), dev(dp_, dq_))
        b = tx.send(src(p, q, None), region(idx(p, q), None), dev(-dp_, -dq_))
        return a, b

    first = ring(0, 0, "p")
    second = {0: ring(0, 0, "q")}
    yield
    tx.arrived(first[0], region(idx(-1, 0), None), dev(1, 0))
    o0 = tx.send(region(idx(-1, 0), 0), region(idx(-1, 0), 0), dev(1, 0))
    second[-1] = ring(-1, 0, "q")
    tx.arrived(first[1], region(idx(1, 0), None), dev(-1, 0))
    o1 = tx.send(region(idx(1, 0), 1), region(idx(1, 0), 1), dev(-1, 0))
    second[1] = ring(1, 0, "q")
    yield
    tx.arrived(o0, region(idx(2, 0), 0), dev(1, 0))
    tx.arrived(o1, region(idx(2, 0), 1), dev(-1, 0))
    second[2] = ring(2, 0, "q")
    yield
    last = []
    for p in (0, -1, 1, 2):
        a, b = second[p]
        tx.arrived(a, region(idx(p, -1), None), dev(0, 1))
        last.append((tx.send(region(idx(p, -1), 0), region(idx(p, -1), 0), dev(0, 1)), p, 0))
        tx.arrived(b, region(idx(p, 1), None), dev(0, -1))
        last.append((tx.send(region(idx(p, 1), 1), region(idx(p, 1), 1), dev(0, -1)), p, 1))
        if p == -1:
            yield
    yield
    for n, p, h in last:
        tx.arrived(n, region(idx(p, 2), h), dev(0, 1))
    yield


SENDS1 = 6 * 20 + 2 * 17


def collect_kernel(gate, up, down, tok, meta, gate_o, up_o, down_o, tok_o, meta_o,
                   st_g, st_u, st_d, st_t, st_m, send_sem, recv_sem, loc_sem):
    me = Place()
    tx = Sender(send_sem, recv_sem)
    stage = ((gate, st_g), (up, st_u), (down, st_d), (tok, st_t), (meta, st_m))
    loads = [pltpu.make_async_copy(a, b, loc_sem.at[i]) for i, (a, b) in enumerate(stage)]
    for cp in loads:
        cp.start()
    barrier([me.dev_xy(1, 0), me.dev_xy(-1, 0), me.dev_xy(0, 1), me.dev_xy(0, -1),
             me.dev_z(1), me.dev_z(-1), me.partner()])

    def block_region(ref, size):
        def region(z, c, h):
            v = ref.at[z * 2 + c]
            return v if h is None else v.at[pl.ds(h * (size // 2), size // 2)]
        return region

    def rows_region(ref, e):
        n = WIDTH // GROUP

        def region(dp, h):
            if h is None:
                return ref.at[e, pl.ds(pl.multiple_of(dp * n, n), n), :]
            return ref.at[e, pl.ds(pl.multiple_of(dp * n + h * (n // 2), n // 2), n // 2), :]
        return region

    def cols_region(ref, e):
        n = WIDTH // GROUP

        def region(dp, h):
            cols = pl.ds(pl.multiple_of(dp * n, n), n)
            if h is None:
                return ref.at[e, :, cols]
            return ref.at[e, pl.ds(h * (HIDDEN // 2), HIDDEN // 2), cols]
        return region

    def own_half(ref, e):
        def own(h):
            v = ref.at[e]
            n = v.shape[0] // 2
            return v if h is None else v.at[pl.ds(h * n, n)]
        return own

    def jobs(ref, region_of, out):
        return [gather_xy(me, tx, own_half(ref, e), region_of(out, e), e == 0) for e in (0, 1)]

    meta_j = gather_z(me, tx, meta, block_region(meta_o, 16))
    tok_j = gather_z(me, tx, tok, block_region(tok_o, BLOCK))
    w_j = [jobs(gate, rows_region, gate_o), jobs(up, rows_region, up_o), jobs(down, cols_region, down_o)]

    def step(js):
        for j in js:
            next(j, None)

    step([meta_j])
    step(w_j[0])
    step([tok_j])
    step(w_j[1])
    outs = (gate_o.at[:, pl.ds(pl.multiple_of(me.dp * BLOCK, BLOCK), BLOCK), :],
            up_o.at[:, pl.ds(pl.multiple_of(me.dp * BLOCK, BLOCK), BLOCK), :],
            down_o.at[:, :, pl.ds(pl.multiple_of(me.dp * BLOCK, BLOCK), BLOCK)],
            tok_o.at[me.ex], meta_o.at[me.ex])
    stores = []
    for i, cp in enumerate(loads):
        cp.wait()
        stores.append(pltpu.make_async_copy(stage[i][1], outs[i], loc_sem.at[5 + i]))
        stores[-1].start()
    step(w_j[2])
    for _ in range(8):
        step(w_j[0])
        step([meta_j, tok_j])
        step(w_j[1])
        step(w_j[2])
    for cp in stores:
        cp.wait()
    tx.finish()


def collect(gate, up, down, tok, meta):
    sds = jax.ShapeDtypeStruct
    return pl.pallas_call(
        collect_kernel,
        out_shape=(sds((2, WIDTH, HIDDEN), BF), sds((2, WIDTH, HIDDEN), BF), sds((2, HIDDEN, WIDTH), BF),
                   sds((GROUP, BLOCK, WIDTH), BF), sds((GROUP, 16, BLOCK), F32)),
        in_specs=[ANY] * 5,
        out_specs=(ANY,) * 5,
        scratch_shapes=[pltpu.VMEM(a.shape, a.dtype) for a in (gate, up, down, tok, meta)]
        + [pltpu.SemaphoreType.DMA((SENDS1,)), pltpu.SemaphoreType.DMA((SENDS1,)), pltpu.SemaphoreType.DMA((10,))],
        compiler_params=pltpu.CompilerParams(collective_id=0, has_side_effects=True),
        name="collect",
    )(gate, up, down, tok, meta)


def split2(v):
    hi = v.astype(BF)
    return hi, (v - hi.astype(F32)).astype(BF)


def dot(a, b):
    return jnp.dot(a, b, preferred_element_type=F32)


def tables(meta):
    ex = lax.axis_index("expert").astype(F32)
    row = lax.broadcasted_iota(jnp.int32, (BLOCK, BLOCK), 0)
    col = lax.broadcasted_iota(jnp.int32, (BLOCK, BLOCK), 1)
    before = (row < col).astype(BF)
    quarter = lax.rem(lax.broadcasted_iota(jnp.int32, (GROUP, BLOCK), 0), 4).astype(F32)

    def one(ids, shares, which, cap):
        hit = (ids == which).astype(F32)
        named = jnp.sum(hit, axis=1)
        share = jnp.sum(hit * shares, axis=1)
        pos = dot(named.astype(BF), before) + quarter * cap
        return jnp.where(named > 0, pos, -1.0), share

    fid, pid, fsh, psh = (meta[:, 4 * i:4 * i + 4, :] for i in range(4))
    a = one(fid, fsh, 2.0 * ex, CAPF)
    b = one(fid, fsh, 2.0 * ex + 1.0, CAPF)
    p = one(pid, psh, ex, CAPP)
    return a, b, p


def quad_row(v, q):
    return jnp.concatenate([v[4 * q + i:4 * q + i + 1, :] for i in range(4)], axis=1)


def quad_col(v, first, q):
    return jnp.concatenate([v[:, first + 4 * q + i:first + 4 * q + i + 1] for i in range(4)], axis=0)


def pick(rows, pos):
    slot = lax.broadcasted_iota(jnp.int32, (rows, TOKQ), 0).astype(F32)
    return (slot == pos).astype(BF)


def put(rows, pos, share):
    slot = lax.broadcasted_iota(jnp.int32, (TOKQ, rows), 1).astype(F32)
    return jnp.where(slot == pos, share, 0.0)


def experts_kernel(gate_h, up_h, down_h, tok_h, meta, first, second, part_h, hid_o, low_o,
                   gate, up, down, tok, x0, x1, h0, h1, wt, low3, b3, rows, outb, sems, out_sem):
    loads = []
    for q in range(QUADS):
        loads.append(pltpu.make_async_copy(tok_h.at[pl.ds(4 * q, 4)], tok.at[pl.ds(4 * q, 4)], sems.at[q]))
    for i, (s, d) in enumerate(((gate_h, gate), (up_h, up), (down_h, down))):
        loads.append(pltpu.make_async_copy(s, d, sems.at[QUADS + i]))
    for cp in loads:
        cp.start()

    (pa, wa), (pb, wb), (pp, wp) = tables(meta[...])
    cols = jnp.transpose(jnp.concatenate([pa, pb, pp, -wa, -wb, wp, pp, wp], axis=0))
    for q in range(QUADS):
        wt[q] = jnp.concatenate([
            put(RF, quad_col(cols, 0, q), quad_col(cols, 48, q)),
            put(RP, quad_col(cols, 32, q), quad_col(cols, 80, q)),
            put(RF, quad_col(cols, 16, q), quad_col(cols, 64, q)),
        ], axis=1).astype(BF)
    bh, bl = split2(second[0])
    b3[0:RANK], b3[RANK:2 * RANK], b3[2 * RANK:] = bh, bh, bl

    for q in range(QUADS):
        loads[q].wait()
        oa, op, ob = pick(RF, quad_row(pa, q)), pick(RP, quad_row(pp, q)), pick(RF, quad_row(pb, q))

        def gather(i, _):
            at = pl.ds(pl.multiple_of(i * 512, 512), 512)
            t = tok[4 * q:4 * q + 4, :, at].reshape(TOKQ, 512)
            x0[q * RF:(q + 1) * RF, at] = dot(oa, t).astype(BF)
            x0[QUADS * RF + q * RP:QUADS * RF + (q + 1) * RP, at] = dot(op, t).astype(BF)
            x1[q * RF:(q + 1) * RF, at] = dot(ob, t).astype(BF)
            return 0

        lax.fori_loop(0, 4, gather, 0)

    loads[QUADS].wait()
    loads[QUADS + 1].wait()

    def hidden(x, h, e, m, n):
        rows_m = x.shape[0] // m

        def body(i, _):
            rr = pl.ds(pl.multiple_of(lax.rem(i, m) * rows_m, rows_m), rows_m)
            cc = pl.ds(pl.multiple_of(lax.div(i, m) * n, n), n)
            g = dot(x[rr, :], gate[e, :, cc])
            u = dot(x[rr, :], up[e, :, cc])
            h[rr, cc] = (g / (1.0 + jnp.exp(-g)) * u).astype(BF)
            return 0

        lax.fori_loop(0, m * (HIDDEN // n), body, 0)

    hidden(x0, h0, 0, 2, CHUNK)
    hidden(x1, h1, 1, 1, CHUNK)

    hid = h0[QUADS * RF:, :]
    ah, al = split2(first[0])
    low2 = dot(hid, jnp.concatenate([ah, al], axis=1))
    low = low2[:, :RANK] + low2[:, RANK:]
    lh, ll = split2(low)
    low3[...] = jnp.concatenate([lh, ll, lh], axis=1)
    hid_o[...] = hid
    low_o[...] = low
    loads[QUADS + 2].wait()

    def out_copy(i, slot):
        at = pl.ds(pl.multiple_of(i * CHUNK, CHUNK), CHUNK)
        return pltpu.make_async_copy(outb.at[slot], part_h.at[:, at], out_sem.at[slot])

    def down_step(i, _):
        at = pl.ds(pl.multiple_of(i * CHUNK, CHUNK), CHUNK)
        slot = lax.rem(i, 2)
        r0 = dot(h0[...], down[0, :, at])
        rp = r0[QUADS * RF:] + dot(low3[...], b3[:, at])
        r1 = dot(h1[...], down[1, :, at])
        for q in range(QUADS):
            rows[q, 0:RF] = r0[q * RF:(q + 1) * RF].astype(BF)
            rows[q, RF:RF + RP] = rp[q * RP:(q + 1) * RP].astype(BF)
            rows[q, RF + RP:] = r1[q * RF:(q + 1) * RF].astype(BF)

        @pl.when(i >= 2)
        def _():
            out_copy(i - 2, slot).wait()

        for q in range(QUADS):
            outb[slot, q * TOKQ:(q + 1) * TOKQ, :] = dot(wt[q], rows[q]).astype(BF)
        out_copy(i, slot).start()
        return 0

    steps = WIDTH // CHUNK
    lax.fori_loop(0, steps, down_step, 0)
    for i in (steps - 2, steps - 1):
        out_copy(i, i % 2).wait()


def experts(gate, up, down, tok, meta, first, second):
    sds = jax.ShapeDtypeStruct
    vm = pltpu.VMEM
    return pl.pallas_call(
        experts_kernel,
        out_shape=(sds((GROUP * BLOCK, WIDTH), BF), sds((QUADS * RP, HIDDEN), BF), sds((QUADS * RP, RANK), F32)),
        in_specs=[ANY] * 4 + [VM] * 3,
        out_specs=(ANY, VM, VM),
        scratch_shapes=[
            vm(gate.shape, BF), vm(up.shape, BF), vm(down.shape, BF), vm(tok.shape, BF),
            vm((ROWS0, WIDTH), BF), vm((ROWS1, WIDTH), BF), vm((ROWS0, HIDDEN), BF), vm((ROWS1, HIDDEN), BF),
            vm((QUADS, TOKQ, RQ), BF), vm((QUADS * RP, 3 * RANK), BF), vm((3 * RANK, WIDTH), BF),
            vm((QUADS, RQ, CHUNK), BF), vm((2, GROUP * BLOCK, CHUNK), BF),
            pltpu.SemaphoreType.DMA((QUADS + 3,)), pltpu.SemaphoreType.DMA((2,)),
        ],
        compiler_params=pltpu.CompilerParams(vmem_limit_bytes=60 << 20),
        name="experts",
    )(gate, up, down, tok, meta, first, second)


SENDS3 = 8 + 14 + 17


def reduce_kernel(part, out, mine, theirs, ring, own, send_sem, recv_sem, loc_sem):
    me = Place()
    tx = Sender(send_sem, recv_sem)
    half = BLOCK // 2
    order = (4, 3, -3, 2, -2, 1, -1, 0)
    loads = {}
    for i, k in enumerate(order):
        loads[k] = pltpu.make_async_copy(part.at[me.zz(k) * 2 + me.c], mine.at[me.zz(k)], loc_sem.at[i])
        loads[k].start()
    barrier([me.dev_z(1), me.dev_z(-1), me.partner()])
    swap = {}
    for k in order:
        swap[k] = tx.send(part.at[me.zz(k) * 2 + 1 - me.c], theirs.at[me.zz(k)], me.partner())

    def pair_sum(k):
        loads[k].wait()
        tx.arrived(swap[k], theirs.at[me.zz(k)], me.partner())
        d = me.zz(k)
        mine[d] = (mine[d].astype(F32) + theirs[d].astype(F32)).astype(BF)

    def rows(h):
        return pl.ds(h * half, half)

    slot = {}
    waiting = {}

    def push(sign, h, j):
        d = me.zz(sign * j)
        key = (sign, h)
        if key in waiting:
            n, s = waiting[key]
            tx.arrived(n, ring.at[s], me.dev_z(sign))
            mine[d, rows(h)] = (mine[d, rows(h)].astype(F32) + ring[s].astype(F32)).astype(BF)
        s = slot.setdefault((sign, h, j), len(slot))
        waiting[key] = (tx.send(mine.at[d, rows(h)], ring.at[s], me.dev_z(sign)), s)

    pair_sum(4)
    push(1, 0, 4)
    push(-1, 1, 4)
    for j in (3, 2, 1):
        pair_sum(j)
        pair_sum(-j)
        push(1, 1, j)
        push(-1, 0, j)
        push(1, 0, j)
        push(-1, 1, j)
    pair_sum(0)
    for h in (1, 0):
        total = mine[me.z, rows(h)].astype(F32)
        for sign in (1, -1):
            n, s = waiting[(sign, h)]
            tx.arrived(n, ring.at[s], me.dev_z(sign))
            total = total + ring[s].astype(F32)
        own[rows(h)] = total.astype(BF)

    def region(z, c, h):
        v = out.at[z * 2 + c]
        return v if h is None else v.at[rows(h)]

    last = pltpu.make_async_copy(own, out.at[me.ex], loc_sem.at[8])
    last.start()
    for _ in gather_z(me, tx, own, region):
        pass
    last.wait()
    tx.finish()


def reduce_residual(part):
    vm = pltpu.VMEM
    return pl.pallas_call(
        reduce_kernel,
        out_shape=jax.ShapeDtypeStruct((GROUP, BLOCK, WIDTH), BF),
        in_specs=[ANY],
        out_specs=ANY,
        scratch_shapes=[
            vm((NZ, BLOCK, WIDTH), BF), vm((NZ, BLOCK, WIDTH), BF), vm((14, BLOCK // 2, WIDTH), BF),
            vm((BLOCK, WIDTH), BF),
            pltpu.SemaphoreType.DMA((SENDS3,)), pltpu.SemaphoreType.DMA((SENDS3,)), pltpu.SemaphoreType.DMA((9,)),
        ],
        compiler_params=pltpu.CompilerParams(collective_id=1, has_side_effects=True),
        name="reduce_residual",
    )(part)


def grads_kernel(res_h, meta, hid, low, second, ga_o, gb_o, res, back, sems):
    loads = []
    for q in range(QUADS):
        loads.append(pltpu.make_async_copy(res_h.at[pl.ds(4 * q, 4)], res.at[pl.ds(4 * q, 4)], sems.at[q]))
    for cp in loads:
        cp.start()
    (_, _), (_, _), (pp, wp) = tables(meta[...])
    bh, bl = split2(second[0])
    b2 = jnp.concatenate([bh, bl], axis=0)
    nt = (((1,), (1,)), ((), ()))
    tn = (((0,), (0,)), ((), ()))
    gb = jnp.zeros((2 * RANK, WIDTH), F32)
    for q in range(QUADS):
        op = pick(RP, quad_row(pp, q))
        share = quad_row(wp, q)
        lq = low[q * RP:(q + 1) * RP, :]
        l1 = lq.astype(BF)
        r1 = lq - l1.astype(F32)
        l2 = r1.astype(BF)
        l3 = (r1 - l2.astype(F32)).astype(BF)
        spread = lax.dot_general(jnp.concatenate([l1, l2, l3, jnp.zeros_like(l1)], axis=1), op, tn,
                                 preferred_element_type=F32)
        low_t = (spread[0:RANK] + spread[RANK:2 * RANK] + spread[2 * RANK:3 * RANK]) * share
        th, tl = split2(low_t)
        loads[q].wait()
        rq = res[4 * q:4 * q + 4].reshape(TOKQ, WIDTH)
        gb = gb + dot(jnp.concatenate([th, tl], axis=0), rq)
        bt = lax.dot_general(b2, rq, nt, preferred_element_type=F32)
        bt = (bt[:RANK] + bt[RANK:]) * share
        b_hi, b_lo = split2(bt)
        picked = lax.dot_general(op, jnp.concatenate([b_hi, b_lo], axis=0), nt, preferred_element_type=F32)
        back[q * RP:(q + 1) * RP, :] = picked.astype(BF)
    gb_o[...] = gb[:RANK] + gb[RANK:]
    ga = lax.dot_general(hid[...], back[...], tn, preferred_element_type=F32)
    ga_o[...] = ga[:, :RANK] + ga[:, RANK:]


def grads(res, meta, hid, low, second):
    sds = jax.ShapeDtypeStruct
    vm = pltpu.VMEM
    return pl.pallas_call(
        grads_kernel,
        out_shape=(sds((HIDDEN, RANK), F32), sds((RANK, WIDTH), F32)),
        in_specs=[ANY] + [VM] * 4,
        out_specs=(VM, VM),
        scratch_shapes=[vm((GROUP, BLOCK, WIDTH), BF), vm((QUADS * RP, 2 * RANK), BF), pltpu.SemaphoreType.DMA((QUADS,))],
        compiler_params=pltpu.CompilerParams(vmem_limit_bytes=60 << 20),
        name="grads",
    )(res, meta, hid, low, second)


def exchange_kernel(pa, pb, ga, gb, ra, rb, send_sem, recv_sem):
    dp, ex = lax.axis_index("dp"), lax.axis_index("expert")
    tx = Sender(send_sem, recv_sem)
    na, nb = HIDDEN // GROUP, WIDTH // GROUP

    def dev(o):
        return (lax.rem(dp + o, GROUP), ex)

    barrier([dev(o) for o in range(1, GROUP)])
    got = []
    for o in range(1, GROUP):
        d = lax.rem(dp + o, GROUP)
        got.append(tx.send(pa.at[pl.ds(pl.multiple_of(d * na, na), na)], ra.at[o - 1], dev(o)))
        got.append(tx.send(pb.at[:, pl.ds(pl.multiple_of(d * nb, nb), nb)], rb.at[o - 1], dev(o)))
    ta = pa[pl.ds(pl.multiple_of(dp * na, na), na), :]
    tb = pb[:, pl.ds(pl.multiple_of(dp * nb, nb), nb)]
    for o in range(1, GROUP):
        tx.arrived(got[2 * o - 2], ra.at[o - 1], dev(o))
        tx.arrived(got[2 * o - 1], rb.at[o - 1], dev(o))
        ta = ta + ra[o - 1]
        tb = tb + rb[o - 1]
    ga[...] = ta
    gb[...] = tb
    tx.finish()


def exchange(pa, pb):
    sds = jax.ShapeDtypeStruct
    vm = pltpu.VMEM
    na, nb = HIDDEN // GROUP, WIDTH // GROUP
    n = 2 * (GROUP - 1)
    return pl.pallas_call(
        exchange_kernel,
        out_shape=(sds((na, RANK), F32), sds((RANK, nb), F32)),
        in_specs=[VM, VM],
        out_specs=(VM, VM),
        scratch_shapes=[
            vm((GROUP - 1, na, RANK), F32), vm((GROUP - 1, RANK, nb), F32),
            pltpu.SemaphoreType.DMA((n,)), pltpu.SemaphoreType.DMA((n,)),
        ],
        compiler_params=pltpu.CompilerParams(collective_id=2, has_side_effects=True),
        name="exchange",
    )(pa, pb)


def shards(tokens, fid, pid, fsc, psc, gate, up, down, first, second):
    fsh = fsc / jnp.sum(fsc, axis=1, keepdims=True)
    psh = psc / jnp.sum(psc, axis=1, keepdims=True)
    meta = jnp.concatenate([fid.astype(F32), pid.astype(F32), fsh, psh], axis=1).T
    gate_f, up_f, down_f, tok_f, meta_f = collect(gate, up, down, tokens, meta)
    part, hid, low = experts(gate_f, up_f, down_f, tok_f, meta_f, first, second)
    res = reduce_residual(part.reshape(GROUP, BLOCK, WIDTH))
    pa, pb = grads(res, meta_f, hid, low, second)
    ga, gb = exchange(pa, pb)
    return ga[None], gb[None]


def solution(mesh):
    rows = P(("dp", "expert"), None)
    return jax.shard_map(
        shards,
        mesh=mesh,
        in_specs=(rows,) * 5 + (P("expert", "dp", None), P("expert", "dp", None), P("expert", None, "dp"),
                                P("expert", None, None), P("expert", None, None)),
        out_specs=(P("expert", "dp", None), P("expert", None, "dp")),
        check_vma=False,
    )
```

```python
import functools

import jax
import jax.numpy as jnp
from jax import lax
from jax.experimental import pallas as pl
from jax.experimental.pallas import tpu as pltpu
from jax.sharding import PartitionSpec as P

BF = jnp.bfloat16
F32 = jnp.float32
MESH = pl.DeviceIdType.MESH
ANY = pl.BlockSpec(memory_space=pl.ANY)
VM = pl.BlockSpec(memory_space=pltpu.VMEM)

NX = 4
NZ = 8
GROUP = 16
BLOCK = 128
WIDTH = 2048
HIDDEN = 768
RANK = 64
QUADS = 4
TOKQ = 4 * BLOCK
CAPF = 18
CAPP = 36
RF = 80
RP = 144
RQ = 2 * RF + RP
ROWS0 = QUADS * (RF + RP)
ROWS1 = QUADS * RF
CHUNK = 256


class Place:
    def __init__(self):
        dp, ex = lax.axis_index("dp"), lax.axis_index("expert")
        self.dp, self.ex = dp, ex
        self.x, self.y = lax.rem(dp, NX), lax.div(dp, NX)
        self.z, self.c = lax.div(ex, 2), lax.rem(ex, 2)

    def xy(self, dx, dy):
        return lax.rem(self.y + dy + NX, NX) * NX + lax.rem(self.x + dx + NX, NX)

    def zz(self, dz):
        return lax.rem(self.z + dz + NZ, NZ)

    def dev_xy(self, dx, dy):
        return (self.xy(dx, dy), self.ex)

    def dev_z(self, dz):
        return (self.dp, self.zz(dz) * 2 + self.c)

    def partner(self):
        return (self.dp, self.z * 2 + 1 - self.c)


def barrier(devices):
    sem = pltpu.get_barrier_semaphore()
    for d in devices:
        pl.semaphore_signal(sem, inc=1, device_id=d, device_id_type=MESH)
    pl.semaphore_wait(sem, len(devices))


class Sender:
    def __init__(self, send_sem, recv_sem):
        self.send_sem, self.recv_sem = send_sem, recv_sem
        self.count = 0
        self.sent = []

    def send(self, src, dst, device):
        n = self.count
        self.count += 1
        cp = pltpu.make_async_remote_copy(
            src_ref=src, dst_ref=dst, send_sem=self.send_sem.at[n], recv_sem=self.recv_sem.at[n],
            device_id=device, device_id_type=MESH,
        )
        cp.start()
        self.sent.append(cp)
        return n

    def arrived(self, n, region, device):
        pltpu.make_async_remote_copy(
            src_ref=region, dst_ref=region, send_sem=self.send_sem.at[n], recv_sem=self.recv_sem.at[n],
            device_id=device, device_id_type=MESH,
        ).wait_recv()

    def finish(self):
        for cp in self.sent:
            cp.wait_send()


def gather_z(me, tx, own, region):
    c = me.c
    half = own.shape[0] // 2

    def part(ref, h):
        return ref if h is None else ref.at[pl.ds(h * half, half)]

    plus = tx.send(own, region(me.z, c, None), me.dev_z(1))
    minus = tx.send(own, region(me.z, c, None), me.dev_z(-1))
    got = [(tx.send(own, region(me.z, c, None), me.partner()), 0, None)]
    yield
    for k in (1, 2, 3):
        zl, zr = me.zz(-k), me.zz(k)
        tx.arrived(plus, region(zl, c, None), me.dev_z(1))
        plus = (tx.send(region(zl, c, None), region(zl, c, None), me.dev_z(1)) if k < 3
                else tx.send(region(zl, c, 0), region(zl, c, 0), me.dev_z(1)))
        got.append((tx.send(region(zl, c, None), region(zl, c, None), me.partner()), -k, None))
        tx.arrived(minus, region(zr, c, None), me.dev_z(-1))
        minus = (tx.send(region(zr, c, None), region(zr, c, None), me.dev_z(-1)) if k < 3
                 else tx.send(region(zr, c, 1), region(zr, c, 1), me.dev_z(-1)))
        got.append((tx.send(region(zr, c, None), region(zr, c, None), me.partner()), k, None))
        yield
    zo = me.zz(4)
    tx.arrived(plus, region(zo, c, 0), me.dev_z(1))
    got.append((tx.send(region(zo, c, 0), region(zo, c, 0), me.partner()), 4, 0))
    tx.arrived(minus, region(zo, c, 1), me.dev_z(-1))
    got.append((tx.send(region(zo, c, 1), region(zo, c, 1), me.partner()), 4, 1))
    yield
    for n, k, h in got:
        tx.arrived(n, region(me.zz(k), 1 - c, h), me.partner())
    yield


def gather_xy(me, tx, own, region, x_first):
    def idx(p, q):
        return me.xy(p, q) if x_first else me.xy(q, p)

    def dev(p, q):
        return me.dev_xy(p, q) if x_first else me.dev_xy(q, p)

    def src(p, q, h):
        return own(h) if (p, q) == (0, 0) else region(idx(p, q), h)

    def ring(p, q, dp_, dq_):
        return (tx.send(src(p, q, None), region(idx(p, q), None), dev(dp_, dq_)),
                tx.send(src(p, q, None), region(idx(p, q), None), dev(-dp_, -dq_)))

    def relay(n, p, q, dp_, dq_, h):
        tx.arrived(n, region(idx(p, q), None), dev(dp_, dq_))
        return tx.send(region(idx(p, q), h), region(idx(p, q), h), dev(dp_, dq_))

    far = {}

    def along_q(p):
        a, b = second[p]
        far[p] = (relay(a, p, -1, 0, 1, 0), relay(b, p, 1, 0, -1, 1))

    def opposite(p):
        for h in (0, 1):
            tx.arrived(far[p][h], region(idx(p, 2), h), dev(0, 1))

    first = ring(0, 0, 1, 0)
    second = {0: ring(0, 0, 0, 1)}
    yield
    o0 = relay(first[0], -1, 0, 1, 0, 0)
    second[-1] = ring(-1, 0, 0, 1)
    o1 = relay(first[1], 1, 0, -1, 0, 1)
    second[1] = ring(1, 0, 0, 1)
    along_q(0)
    yield
    tx.arrived(o0, region(idx(2, 0), 0), dev(1, 0))
    tx.arrived(o1, region(idx(2, 0), 1), dev(-1, 0))
    second[2] = ring(2, 0, 0, 1)
    along_q(-1)
    along_q(1)
    if not x_first:
        opposite(0)
    yield
    along_q(2)
    if not x_first:
        opposite(-1)
        opposite(1)
    yield
    for p in (0, -1, 1, 2) if x_first else (2,):
        opposite(p)
    yield


def split2(v):
    hi = v.astype(BF)
    return hi, (v - hi.astype(F32)).astype(BF)


def dot(a, b):
    return jnp.dot(a, b, preferred_element_type=F32)


def tables(meta):
    ex = lax.axis_index("expert").astype(F32)
    row = lax.broadcasted_iota(jnp.int32, (BLOCK, BLOCK), 0)
    col = lax.broadcasted_iota(jnp.int32, (BLOCK, BLOCK), 1)
    before = (row < col).astype(BF)
    quarter = lax.rem(lax.broadcasted_iota(jnp.int32, (GROUP, BLOCK), 0), 4).astype(F32)

    def one(ids, shares, which, cap):
        hit = (ids == which).astype(F32)
        named = jnp.sum(hit, axis=1)
        share = jnp.sum(hit * shares, axis=1)
        pos = dot(named.astype(BF), before) + quarter * cap
        return jnp.where(named > 0, pos, -1.0), share

    fid, pid, fsh, psh = (meta[:, 4 * i:4 * i + 4, :] for i in range(4))
    a = one(fid, fsh, 2.0 * ex, CAPF)
    b = one(fid, fsh, 2.0 * ex + 1.0, CAPF)
    p = one(pid, psh, ex, CAPP)
    return a, b, p


def quad_row(v, q):
    return jnp.concatenate([v[4 * q + i:4 * q + i + 1, :] for i in range(4)], axis=1)


def quad_col(v, first, q):
    return jnp.concatenate([v[:, first + 4 * q + i:first + 4 * q + i + 1] for i in range(4)], axis=0)


def pick(rows, pos):
    slot = lax.broadcasted_iota(jnp.int32, (rows, TOKQ), 0).astype(F32)
    return (slot == pos).astype(BF)


def put(rows, pos, share):
    slot = lax.broadcasted_iota(jnp.int32, (TOKQ, rows), 1).astype(F32)
    return jnp.where(slot == pos, share, 0.0)


STRIPES = 4
COLS = WIDTH // STRIPES
ORDER = (4, 3, -3, 2, -2, 1, -1, 0)
SENDS = 6 * 20 + 2 * 17 + STRIPES * (8 + 14 + 17)


def reduce_stripe(me, tx, ci, cols, part, theirs, ring, own, out, loc_sem):
    half = BLOCK // 2

    def mine(k, h=None):
        at = slice(None) if h is None else pl.ds(h * half, half)
        return part.at[me.zz(k) * 2 + me.c, at, cols]

    swap = {k: tx.send(part.at[me.zz(k) * 2 + 1 - me.c, :, cols], theirs.at[ci, me.zz(k)], me.partner()) for k in ORDER}
    yield

    def pair_sum(k):
        tx.arrived(swap[k], theirs.at[ci, me.zz(k)], me.partner())
        r = mine(k)
        r[...] = (r[...].astype(F32) + theirs[ci, me.zz(k)].astype(F32)).astype(BF)

    slot, waiting = {}, {}

    def push(sign, h, j):
        r = mine(sign * j, h)
        if (sign, h) in waiting:
            n, s = waiting[(sign, h)]
            tx.arrived(n, ring.at[ci, s], me.dev_z(sign))
            r[...] = (r[...].astype(F32) + ring[ci, s].astype(F32)).astype(BF)
        s = slot.setdefault((sign, h, j), len(slot))
        waiting[(sign, h)] = (tx.send(r, ring.at[ci, s], me.dev_z(sign)), s)

    pair_sum(4)
    push(1, 0, 4)
    push(-1, 1, 4)
    pair_sum(3)
    pair_sum(-3)
    push(1, 1, 3)
    push(-1, 0, 3)
    yield
    for j in (3, 2, 1):
        if j < 3:
            pair_sum(j)
            pair_sum(-j)
            push(1, 1, j)
            push(-1, 0, j)
        push(1, 0, j)
        push(-1, 1, j)
        yield
    pair_sum(0)
    for h in (1, 0):
        total = mine(0, h)[...].astype(F32)
        for sign in (1, -1):
            n, s = waiting[(sign, h)]
            tx.arrived(n, ring.at[ci, s], me.dev_z(sign))
            total = total + ring[ci, s].astype(F32)
        own[ci, pl.ds(h * half, half)] = total.astype(BF)

    def region(z, c, h):
        at = slice(None) if h is None else pl.ds(h * half, half)
        return out.at[z * 2 + c, at, cols]

    last = pltpu.make_async_copy(own.at[ci], out.at[me.ex, :, cols], loc_sem)
    last.start()
    yield from gather_z(me, tx, own.at[ci], region)
    last.wait()
    yield


def main_kernel(gate_i, up_i, down_i, tok_i, meta_i, first, second, res_o, meta_o, hid_o, low_o,
                gate, up, down, tok, meta, x0, x1, acc, h0, h1, wt, low3, b3, rows, theirs, ring, own,
                send_sem, recv_sem, loc_sem):
    me = Place()
    tx = Sender(send_sem, recv_sem)
    mine = pl.ds(pl.multiple_of(me.dp * BLOCK, BLOCK), BLOCK)
    loads = [
        pltpu.make_async_copy(s, d, loc_sem.at[i]) for i, (s, d) in enumerate((
            (meta_i, meta.at[me.ex]), (tok_i, tok.at[me.ex]), (gate_i, gate.at[:, mine, :]),
            (up_i, up.at[:, mine, :]), (down_i, down.at[:, :, mine])))
    ]
    for cp in loads:
        cp.start()
    barrier([me.dev_xy(1, 0), me.dev_xy(-1, 0), me.dev_xy(0, 1), me.dev_xy(0, -1),
             me.dev_z(1), me.dev_z(-1), me.partner()])

    def block_region(ref, size):
        def region(z, c, h):
            v = ref.at[z * 2 + c]
            return v if h is None else v.at[pl.ds(h * (size // 2), size // 2)]
        return region

    def rows_region(ref, e):
        def region(dp, h):
            if h is None:
                return ref.at[e, pl.ds(pl.multiple_of(dp * BLOCK, BLOCK), BLOCK), :]
            n = BLOCK // 2
            return ref.at[e, pl.ds(pl.multiple_of(dp * BLOCK + h * n, n), n), :]
        return region

    def cols_region(ref, e):
        def region(dp, h):
            cols = pl.ds(pl.multiple_of(dp * BLOCK, BLOCK), BLOCK)
            if h is None:
                return ref.at[e, :, cols]
            return ref.at[e, pl.ds(h * (HIDDEN // 2), HIDDEN // 2), cols]
        return region

    def own_half(ref, e):
        def half(h):
            v = ref.at[e]
            n = v.shape[0] // 2
            return v if h is None else v.at[pl.ds(h * n, n)]
        return half

    def jobs(ref, region_of, out):
        return [gather_xy(me, tx, own_half(ref, e), region_of(out, e), e == 0) for e in (0, 1)]

    meta_j = gather_z(me, tx, meta_i, block_region(meta, 16))
    tok_j = gather_z(me, tx, tok_i, block_region(tok, BLOCK))
    gate_j = jobs(gate_i, rows_region, gate)
    up_j = jobs(up_i, rows_region, up)
    down_j = jobs(down_i, cols_region, down)

    def step(*js):
        for j in js:
            next(j, None)

    step(meta_j)
    step(*gate_j)
    step(tok_j)
    step(*up_j)
    bh, bl = split2(second[0])
    b3[0:RANK], b3[RANK:2 * RANK], b3[2 * RANK:] = bh, bh, bl
    step(*gate_j)
    step(meta_j, tok_j)
    step(*up_j)
    step(*gate_j)
    step(meta_j, tok_j)
    step(*up_j)
    step(meta_j, tok_j)
    step(*gate_j)
    step(meta_j, tok_j)
    tok_last = tx.count
    step(meta_j, tok_j)
    step(*up_j)
    step(*down_j)
    for cp in loads:
        cp.wait()

    tab = tables(meta[...])
    (pa, wa), (pb, wb), (pp, wp) = tab
    turned = jnp.transpose(jnp.concatenate([pa, pb, pp, -wa, -wb, wp, pp, wp], axis=0))
    for q in range(QUADS):
        wt[q] = jnp.concatenate([
            put(RF, quad_col(turned, 0, q), quad_col(turned, 48, q)),
            put(RP, quad_col(turned, 32, q), quad_col(turned, 80, q)),
            put(RF, quad_col(turned, 16, q), quad_col(turned, 64, q)),
        ], axis=1).astype(BF)

    for q in range(QUADS):
        oa, op, ob = pick(RF, quad_row(pa, q)), pick(RP, quad_row(pp, q)), pick(RF, quad_row(pb, q))

        def gather(i, _):
            at = pl.ds(pl.multiple_of(i * 512, 512), 512)
            t = tok[4 * q:4 * q + 4, :, at].reshape(TOKQ, 512)
            x0[q * RF:(q + 1) * RF, at] = dot(oa, t).astype(BF)
            x0[QUADS * RF + q * RP:QUADS * RF + (q + 1) * RP, at] = dot(op, t).astype(BF)
            x1[q * RF:(q + 1) * RF, at] = dot(ob, t).astype(BF)
            return 0

        lax.fori_loop(0, 4, gather, 0)

    def stripe(r):
        return pl.ds(pl.multiple_of(lax.rem(me.y + r + NX, NX) * COLS, COLS), COLS)

    def early(x, e, m, first_row):
        rows_m = x.shape[0] // m

        def body(i, _):
            lo = pl.multiple_of(lax.rem(i, m) * rows_m, rows_m)
            rr = pl.ds(lo, rows_m)
            ra = pl.ds(first_row + lo, rows_m)
            cc = pl.ds(pl.multiple_of(lax.div(i, m) * CHUNK, CHUNK), CHUNK)
            for w, ref in enumerate((gate, up)):
                acc[w, ra, cc] = sum(dot(x[rr, stripe(r)], ref[e, stripe(r), cc]) for r in (0, -1, 1))
            return 0

        lax.fori_loop(0, m * (HIDDEN // CHUNK), body, 0)

    def late(x, h, e, m, first_row):
        rows_m = x.shape[0] // m

        def body(i, _):
            lo = pl.multiple_of(lax.rem(i, m) * rows_m, rows_m)
            rr = pl.ds(lo, rows_m)
            ra = pl.ds(first_row + lo, rows_m)
            cc = pl.ds(pl.multiple_of(lax.div(i, m) * CHUNK, CHUNK), CHUNK)
            g = acc[0, ra, cc] + dot(x[rr, stripe(2)], gate[e, stripe(2), cc])
            u = acc[1, ra, cc] + dot(x[rr, stripe(2)], up[e, stripe(2), cc])
            h[rr, cc] = (g / (1.0 + jnp.exp(-g)) * u).astype(BF)
            return 0

        lax.fori_loop(0, m * (HIDDEN // CHUNK), body, 0)

    early(x0, 0, 2, 0)
    early(x1, 1, 1, ROWS0)
    step(*gate_j)
    step(*up_j)
    step(*down_j)
    late(x0, h0, 0, 2, 0)
    late(x1, h1, 1, 1, ROWS0)
    step(*down_j)

    hid = h0[QUADS * RF:, :]
    ah, al = split2(first[0])
    low2 = dot(hid, jnp.concatenate([ah, al], axis=1))
    low = low2[:, :RANK] + low2[:, RANK:]
    lh, ll = split2(low)
    low3[...] = jnp.concatenate([lh, ll, lh], axis=1)
    hid_o[...] = hid
    low_o[...] = low
    meta_o[...] = meta[...]
    for cp in tx.sent[:tok_last]:
        cp.wait_send()
    del tx.sent[:tok_last]

    def partial(r):
        base = lax.rem(me.y + r + NX, NX) * COLS

        def body(i, _):
            at = pl.ds(pl.multiple_of(base + i * CHUNK, CHUNK), CHUNK)
            r0 = dot(h0[...], down[0, :, at])
            rp = r0[QUADS * RF:] + dot(low3[...], b3[:, at])
            r1 = dot(h1[...], down[1, :, at])
            for q in range(QUADS):
                rows[q, 0:RF] = r0[q * RF:(q + 1) * RF].astype(BF)
                rows[q, RF:RF + RP] = rp[q * RP:(q + 1) * RP].astype(BF)
                rows[q, RF + RP:] = r1[q * RF:(q + 1) * RF].astype(BF)
            for q in range(QUADS):
                tok[4 * q:4 * q + 4, :, at] = dot(wt[q], rows[q]).astype(BF).reshape(4, BLOCK, CHUNK)
            return 0

        lax.fori_loop(0, COLS // CHUNK, body, 0)

    red = [reduce_stripe(me, tx, i, stripe(r), tok, theirs, ring, own, res_o, loc_sem.at[5 + i])
           for i, r in enumerate((0, -1, 1, 2))]
    partial(0)
    step(red[0])
    step(*down_j)
    partial(-1)
    step(red[1], red[0])
    partial(1)
    step(red[0], red[2], red[1])
    step(*down_j)
    partial(2)
    step(red[3])
    for _ in range(14):
        step(*red)
    assert tx.count == SENDS
    tx.finish()


def main_call(gate, up, down, tok, meta, first, second):
    sds = jax.ShapeDtypeStruct
    vm = pltpu.VMEM
    return pl.pallas_call(
        main_kernel,
        out_shape=(sds((GROUP, BLOCK, WIDTH), BF), sds((GROUP, 16, BLOCK), F32),
                   sds((QUADS * RP, HIDDEN), BF), sds((QUADS * RP, RANK), F32)),
        in_specs=[ANY] * 5 + [VM] * 2,
        out_specs=(ANY, VM, VM, VM),
        scratch_shapes=[
            vm((2, WIDTH, HIDDEN), BF), vm((2, WIDTH, HIDDEN), BF), vm((2, HIDDEN, WIDTH), BF),
            vm((GROUP, BLOCK, WIDTH), BF), vm((GROUP, 16, BLOCK), F32),
            vm((ROWS0, WIDTH), BF), vm((ROWS1, WIDTH), BF), vm((2, ROWS0 + ROWS1, HIDDEN), F32),
            vm((ROWS0, HIDDEN), BF), vm((ROWS1, HIDDEN), BF),
            vm((QUADS, TOKQ, RQ), BF), vm((QUADS * RP, 3 * RANK), BF), vm((3 * RANK, WIDTH), BF),
            vm((QUADS, RQ, CHUNK), BF),
            vm((STRIPES, NZ, BLOCK, COLS), BF), vm((STRIPES, 14, BLOCK // 2, COLS), BF), vm((STRIPES, BLOCK, COLS), BF),
            pltpu.SemaphoreType.DMA((SENDS,)), pltpu.SemaphoreType.DMA((SENDS,)), pltpu.SemaphoreType.DMA((9,)),
        ],
        compiler_params=pltpu.CompilerParams(collective_id=0, has_side_effects=True, vmem_limit_bytes=62 << 20),
        name="main",
    )(gate, up, down, tok, meta, first, second)


def grads_kernel(res_h, meta, hid, low, second, ga_o, gb_o, res, back, sems):
    loads = []
    for q in range(QUADS):
        loads.append(pltpu.make_async_copy(res_h.at[pl.ds(4 * q, 4)], res.at[pl.ds(4 * q, 4)], sems.at[q]))
    for cp in loads:
        cp.start()
    (_, _), (_, _), (pp, wp) = tables(meta[...])
    bh, bl = split2(second[0])
    b2 = jnp.concatenate([bh, bl], axis=0)
    nt = (((1,), (1,)), ((), ()))
    tn = (((0,), (0,)), ((), ()))
    gb = jnp.zeros((2 * RANK, WIDTH), F32)
    for q in range(QUADS):
        op = pick(RP, quad_row(pp, q))
        share = quad_row(wp, q)
        lq = low[q * RP:(q + 1) * RP, :]
        l1 = lq.astype(BF)
        r1 = lq - l1.astype(F32)
        l2 = r1.astype(BF)
        l3 = (r1 - l2.astype(F32)).astype(BF)
        spread = lax.dot_general(jnp.concatenate([l1, l2, l3, jnp.zeros_like(l1)], axis=1), op, tn,
                                 preferred_element_type=F32)
        low_t = (spread[0:RANK] + spread[RANK:2 * RANK] + spread[2 * RANK:3 * RANK]) * share
        th, tl = split2(low_t)
        loads[q].wait()
        rq = res[4 * q:4 * q + 4].reshape(TOKQ, WIDTH)
        gb = gb + dot(jnp.concatenate([th, tl], axis=0), rq)
        bt = lax.dot_general(b2, rq, nt, preferred_element_type=F32)
        bt = (bt[:RANK] + bt[RANK:]) * share
        b_hi, b_lo = split2(bt)
        picked = lax.dot_general(op, jnp.concatenate([b_hi, b_lo], axis=0), nt, preferred_element_type=F32)
        back[q * RP:(q + 1) * RP, :] = picked.astype(BF)
    gb_o[...] = gb[:RANK] + gb[RANK:]
    ga = lax.dot_general(hid[...], back[...], tn, preferred_element_type=F32)
    ga_o[...] = ga[:, :RANK] + ga[:, RANK:]


def grads(res, meta, hid, low, second):
    sds = jax.ShapeDtypeStruct
    vm = pltpu.VMEM
    return pl.pallas_call(
        grads_kernel,
        out_shape=(sds((HIDDEN, RANK), F32), sds((RANK, WIDTH), F32)),
        in_specs=[ANY] + [VM] * 4,
        out_specs=(VM, VM),
        scratch_shapes=[vm((GROUP, BLOCK, WIDTH), BF), vm((QUADS * RP, 2 * RANK), BF), pltpu.SemaphoreType.DMA((QUADS,))],
        compiler_params=pltpu.CompilerParams(vmem_limit_bytes=60 << 20),
        name="grads",
    )(res, meta, hid, low, second)


def exchange_kernel(pa, pb, ga, gb, ra, rb, send_sem, recv_sem):
    dp, ex = lax.axis_index("dp"), lax.axis_index("expert")
    tx = Sender(send_sem, recv_sem)
    na, nb = HIDDEN // GROUP, WIDTH // GROUP

    def dev(o):
        return (lax.rem(dp + o, GROUP), ex)

    barrier([dev(o) for o in range(1, GROUP)])
    got = []
    for o in range(1, GROUP):
        d = lax.rem(dp + o, GROUP)
        got.append(tx.send(pa.at[pl.ds(pl.multiple_of(d * na, na), na)], ra.at[o - 1], dev(o)))
        got.append(tx.send(pb.at[:, pl.ds(pl.multiple_of(d * nb, nb), nb)], rb.at[o - 1], dev(o)))
    ta = pa[pl.ds(pl.multiple_of(dp * na, na), na), :]
    tb = pb[:, pl.ds(pl.multiple_of(dp * nb, nb), nb)]
    for o in range(1, GROUP):
        tx.arrived(got[2 * o - 2], ra.at[o - 1], dev(o))
        tx.arrived(got[2 * o - 1], rb.at[o - 1], dev(o))
        ta = ta + ra[o - 1]
        tb = tb + rb[o - 1]
    ga[...] = ta
    gb[...] = tb
    tx.finish()


def exchange(pa, pb):
    sds = jax.ShapeDtypeStruct
    vm = pltpu.VMEM
    na, nb = HIDDEN // GROUP, WIDTH // GROUP
    n = 2 * (GROUP - 1)
    return pl.pallas_call(
        exchange_kernel,
        out_shape=(sds((na, RANK), F32), sds((RANK, nb), F32)),
        in_specs=[VM, VM],
        out_specs=(VM, VM),
        scratch_shapes=[
            vm((GROUP - 1, na, RANK), F32), vm((GROUP - 1, RANK, nb), F32),
            pltpu.SemaphoreType.DMA((n,)), pltpu.SemaphoreType.DMA((n,)),
        ],
        compiler_params=pltpu.CompilerParams(collective_id=2, has_side_effects=True),
        name="exchange",
    )(pa, pb)


def shards(tokens, fid, pid, fsc, psc, gate, up, down, first, second):
    fsh = fsc / jnp.sum(fsc, axis=1, keepdims=True)
    psh = psc / jnp.sum(psc, axis=1, keepdims=True)
    meta = jnp.concatenate([fid.astype(F32), pid.astype(F32), fsh, psh], axis=1).T
    res, meta_f, hid, low = main_call(gate, up, down, tokens, meta, first, second)
    pa, pb = grads(res, meta_f, hid, low, second)
    ga, gb = exchange(pa, pb)
    return ga[None], gb[None]


def solution(mesh):
    rows = P(("dp", "expert"), None)
    return jax.shard_map(
        shards,
        mesh=mesh,
        in_specs=(rows,) * 5 + (P("expert", "dp", None), P("expert", "dp", None), P("expert", None, "dp"),
                                P("expert", None, None), P("expert", None, None)),
        out_specs=(P("expert", "dp", None), P("expert", None, "dp")),
        check_vma=False,
    )
```

```python
import functools

import jax
import jax.numpy as jnp
from jax import lax
from jax.experimental import pallas as pl
from jax.experimental.pallas import tpu as pltpu
from jax.sharding import PartitionSpec as P

BF = jnp.bfloat16
F32 = jnp.float32
MESH = pl.DeviceIdType.MESH
ANY = pl.BlockSpec(memory_space=pl.ANY)
VM = pl.BlockSpec(memory_space=pltpu.VMEM)

NX = 4
NZ = 8
GROUP = 16
BLOCK = 128
WIDTH = 2048
HIDDEN = 768
RANK = 64
QUADS = 4
TOKQ = 4 * BLOCK
CAPF = 18
CAPP = 36
RF = 80
RP = 144
RQ = 2 * RF + RP
ROWS0 = QUADS * (RF + RP)
ROWS1 = QUADS * RF
CHUNK = 256


class Place:
    def __init__(self):
        dp, ex = lax.axis_index("dp"), lax.axis_index("expert")
        self.dp, self.ex = dp, ex
        self.x, self.y = lax.rem(dp, NX), lax.div(dp, NX)
        self.z, self.c = lax.div(ex, 2), lax.rem(ex, 2)

    def xy(self, dx, dy):
        return lax.rem(self.y + dy + NX, NX) * NX + lax.rem(self.x + dx + NX, NX)

    def zz(self, dz):
        return lax.rem(self.z + dz + NZ, NZ)

    def dev_xy(self, dx, dy):
        return (self.xy(dx, dy), self.ex)

    def dev_z(self, dz):
        return (self.dp, self.zz(dz) * 2 + self.c)

    def partner(self):
        return (self.dp, self.z * 2 + 1 - self.c)


def barrier(devices):
    sem = pltpu.get_barrier_semaphore()
    for d in devices:
        pl.semaphore_signal(sem, inc=1, device_id=d, device_id_type=MESH)
    pl.semaphore_wait(sem, len(devices))


class Sender:
    def __init__(self, send_sem, recv_sem):
        self.send_sem, self.recv_sem = send_sem, recv_sem
        self.count = 0
        self.sent = []
        self.tag = None

    def send(self, src, dst, device):
        n = self.count
        self.count += 1
        cp = pltpu.make_async_remote_copy(
            src_ref=src, dst_ref=dst, send_sem=self.send_sem.at[n], recv_sem=self.recv_sem.at[n],
            device_id=device, device_id_type=MESH,
        )
        cp.start()
        self.sent.append((self.tag, cp))
        return n

    def arrived(self, n, region, device):
        pltpu.make_async_remote_copy(
            src_ref=region, dst_ref=region, send_sem=self.send_sem.at[n], recv_sem=self.recv_sem.at[n],
            device_id=device, device_id_type=MESH,
        ).wait_recv()

    def drain(self, tags):
        for tag, cp in self.sent:
            if tag in tags:
                cp.wait_send()
        self.sent = [(tag, cp) for tag, cp in self.sent if tag not in tags]


def gather_z(me, tx, own, region):
    c = me.c
    plus = tx.send(own, region(me.z, c, None), me.dev_z(1))
    minus = tx.send(own, region(me.z, c, None), me.dev_z(-1))
    got = [(tx.send(own, region(me.z, c, None), me.partner()), 0, None)]
    yield
    for k in (1, 2, 3):
        zl, zr = me.zz(-k), me.zz(k)
        tx.arrived(plus, region(zl, c, None), me.dev_z(1))
        plus = (tx.send(region(zl, c, None), region(zl, c, None), me.dev_z(1)) if k < 3
                else tx.send(region(zl, c, 0), region(zl, c, 0), me.dev_z(1)))
        got.append((tx.send(region(zl, c, None), region(zl, c, None), me.partner()), -k, None))
        tx.arrived(minus, region(zr, c, None), me.dev_z(-1))
        minus = (tx.send(region(zr, c, None), region(zr, c, None), me.dev_z(-1)) if k < 3
                 else tx.send(region(zr, c, 1), region(zr, c, 1), me.dev_z(-1)))
        got.append((tx.send(region(zr, c, None), region(zr, c, None), me.partner()), k, None))
        yield
    zo = me.zz(4)
    tx.arrived(plus, region(zo, c, 0), me.dev_z(1))
    got.append((tx.send(region(zo, c, 0), region(zo, c, 0), me.partner()), 4, 0))
    tx.arrived(minus, region(zo, c, 1), me.dev_z(-1))
    got.append((tx.send(region(zo, c, 1), region(zo, c, 1), me.partner()), 4, 1))
    yield
    for n, k, h in got:
        tx.arrived(n, region(me.zz(k), 1 - c, h), me.partner())
    yield


def gather_xy(me, tx, own, region, x_first):
    def idx(p, q):
        return me.xy(p, q) if x_first else me.xy(q, p)

    def dev(p, q):
        return me.dev_xy(p, q) if x_first else me.dev_xy(q, p)

    def src(p, q, h):
        return own(h) if (p, q) == (0, 0) else region(idx(p, q), h)

    def ring(p, q, dp_, dq_):
        return (tx.send(src(p, q, None), region(idx(p, q), None), dev(dp_, dq_)),
                tx.send(src(p, q, None), region(idx(p, q), None), dev(-dp_, -dq_)))

    def relay(n, p, q, dp_, dq_, h):
        tx.arrived(n, region(idx(p, q), None), dev(dp_, dq_))
        return tx.send(region(idx(p, q), h), region(idx(p, q), h), dev(dp_, dq_))

    far = {}

    def along_q(p):
        a, b = second[p]
        far[p] = (relay(a, p, -1, 0, 1, 0), relay(b, p, 1, 0, -1, 1))

    def opposite(p):
        for h in (0, 1):
            tx.arrived(far[p][h], region(idx(p, 2), h), dev(0, 1))

    first = ring(0, 0, 1, 0)
    second = {0: ring(0, 0, 0, 1)}
    yield
    o0 = relay(first[0], -1, 0, 1, 0, 0)
    o1 = relay(first[1], 1, 0, -1, 0, 1)
    second[-1] = ring(-1, 0, 0, 1)
    second[1] = ring(1, 0, 0, 1)
    yield
    along_q(0)
    yield
    tx.arrived(o0, region(idx(2, 0), 0), dev(1, 0))
    tx.arrived(o1, region(idx(2, 0), 1), dev(-1, 0))
    second[2] = ring(2, 0, 0, 1)
    yield
    if not x_first:
        opposite(0)
    yield
    along_q(-1)
    along_q(1)
    yield
    along_q(2)
    yield
    if not x_first:
        opposite(-1)
        opposite(1)
    yield
    for p in (0, -1, 1, 2) if x_first else (2,):
        opposite(p)
    yield


def split2(v):
    hi = v.astype(BF)
    return hi, (v - hi.astype(F32)).astype(BF)


def dot(a, b):
    return jnp.dot(a, b, preferred_element_type=F32)


def tables(meta):
    ex = lax.axis_index("expert").astype(F32)
    row = lax.broadcasted_iota(jnp.int32, (BLOCK, BLOCK), 0)
    col = lax.broadcasted_iota(jnp.int32, (BLOCK, BLOCK), 1)
    before = (row < col).astype(BF)
    quarter = lax.rem(lax.broadcasted_iota(jnp.int32, (GROUP, BLOCK), 0), 4).astype(F32)

    def one(ids, shares, which, cap):
        hit = (ids == which).astype(F32)
        named = jnp.sum(hit, axis=1)
        share = jnp.sum(hit * shares, axis=1)
        pos = dot(named.astype(BF), before) + quarter * cap
        return jnp.where(named > 0, pos, -1.0), share

    fid, pid, fsh, psh = (meta[:, 4 * i:4 * i + 4, :] for i in range(4))
    a = one(fid, fsh, 2.0 * ex, CAPF)
    b = one(fid, fsh, 2.0 * ex + 1.0, CAPF)
    p = one(pid, psh, ex, CAPP)
    return a, b, p


def quad_row(v, q):
    return jnp.concatenate([v[4 * q + i:4 * q + i + 1, :] for i in range(4)], axis=1)


def quad_col(v, first, q):
    return jnp.concatenate([v[:, first + 4 * q + i:first + 4 * q + i + 1] for i in range(4)], axis=0)


def pick(rows, pos):
    slot = lax.broadcasted_iota(jnp.int32, (rows, TOKQ), 0).astype(F32)
    return (slot == pos).astype(BF)


def put(rows, pos, share):
    slot = lax.broadcasted_iota(jnp.int32, (TOKQ, rows), 1).astype(F32)
    return jnp.where(slot == pos, share, 0.0)


STRIPES = 4
COLS = WIDTH // STRIPES
ROW_OF = (0, -1, 1, 2)
ORDER = (4, 3, -3, 2, -2, 1, -1, 0)
SENDS = 6 * 20 + 2 * 17 + STRIPES * (8 + 14 + 17) + 2 * (GROUP - 1)

PLAN = (
    "gummttdgugmmtmtutgmTgutgguQQQQugEgududFuLlWdddPP00dd0P0P101d",
    "0P101P201P21P32013231023132V130231C232C3232C3C",
)


def reduce_stripe(me, tx, ci, cols, part, theirs, ring, out):
    half = BLOCK // 2

    def mine(k, h=None):
        at = slice(None) if h is None else pl.ds(h * half, half)
        return part.at[me.zz(k) * 2 + me.c, at, cols]

    def region(z, c, h):
        lo = (z * 2 + c) * BLOCK
        if h is None:
            return out.at[ci, pl.ds(pl.multiple_of(lo, BLOCK), BLOCK), 0:COLS]
        return out.at[ci, pl.ds(pl.multiple_of(lo + h * half, half), half), 0:COLS]

    swap = {k: tx.send(part.at[me.zz(k) * 2 + 1 - me.c, :, cols], theirs.at[ci, me.zz(k)], me.partner()) for k in ORDER}
    yield

    def pair_sum(k):
        tx.arrived(swap[k], theirs.at[ci, me.zz(k)], me.partner())
        r = mine(k)
        r[...] = (r[...].astype(F32) + theirs[ci, me.zz(k)].astype(F32)).astype(BF)

    slot, waiting = {}, {}

    def push(sign, h, j):
        r = mine(sign * j, h)
        if (sign, h) in waiting:
            n, s = waiting[(sign, h)]
            tx.arrived(n, ring.at[ci, s], me.dev_z(sign))
            r[...] = (r[...].astype(F32) + ring[ci, s].astype(F32)).astype(BF)
        s = slot.setdefault((sign, h, j), len(slot))
        waiting[(sign, h)] = (tx.send(r, ring.at[ci, s], me.dev_z(sign)), s)

    pair_sum(4)
    push(1, 0, 4)
    push(-1, 1, 4)
    pair_sum(3)
    pair_sum(-3)
    push(1, 1, 3)
    push(-1, 0, 3)
    yield
    for j in (3, 2, 1):
        if j < 3:
            pair_sum(j)
            pair_sum(-j)
            push(1, 1, j)
            push(-1, 0, j)
        push(1, 0, j)
        push(-1, 1, j)
        yield
    pair_sum(0)
    for h in (1, 0):
        total = mine(0, h)[...].astype(F32)
        for sign in (1, -1):
            n, s = waiting[(sign, h)]
            tx.arrived(n, ring.at[ci, s], me.dev_z(sign))
            total = total + ring[ci, s].astype(F32)
        region(me.z, me.c, h)[...] = total.astype(BF)
    yield from gather_z(me, tx, region(me.z, me.c, None), region)


def main_kernel(gate_i, up_i, down_i, tok_i, fid_i, pid_i, fsc_i, psc_i, first, second, ga_o, gb_o,
                big, down, tok, meta, x0, x1, acc, h0, h1, wt, low_s, low3, b3, rows, theirs, ring,
                sel, low_t, bt, hid_t, back, gbuf, gabuf, ra, rb, send_sem, recv_sem, loc_sem):
    me = Place()
    tx = Sender(send_sem, recv_sem)
    mine = pl.ds(pl.multiple_of(me.dp * BLOCK, BLOCK), BLOCK)
    loads = [
        pltpu.make_async_copy(s, d, loc_sem.at[i]) for i, (s, d) in enumerate((
            (tok_i, tok.at[me.ex]), (gate_i, big.at[0:2, mine, :]),
            (up_i, big.at[2:4, mine, :]), (down_i, down.at[:, :, mine])))
    ]
    for cp in loads:
        cp.start()
    peers = [(dx, dy) for dy in ROW_OF for dx in range(NX)]
    barrier([me.dev_xy(*p) for p in peers if p != (0, 0)] + [me.dev_z(1), me.dev_z(-1), me.partner()])

    def block_region(ref, size):
        def region(z, c, h):
            v = ref.at[z * 2 + c]
            return v if h is None else v.at[pl.ds(h * (size // 2), size // 2)]
        return region

    def rows_region(i):
        def region(dp, h):
            if h is None:
                return big.at[i, pl.ds(pl.multiple_of(dp * BLOCK, BLOCK), BLOCK), :]
            n = BLOCK // 2
            return big.at[i, pl.ds(pl.multiple_of(dp * BLOCK + h * n, n), n), :]
        return region

    def cols_region(e):
        def region(dp, h):
            cols = pl.ds(pl.multiple_of(dp * BLOCK, BLOCK), BLOCK)
            if h is None:
                return down.at[e, :, cols]
            return down.at[e, pl.ds(h * (HIDDEN // 2), HIDDEN // 2), cols]
        return region

    def own_half(ref, e):
        def half(h):
            v = ref.at[e]
            n = v.shape[0] // 2
            return v if h is None else v.at[pl.ds(h * n, n)]
        return half

    def stripe(r):
        return pl.ds(pl.multiple_of(lax.rem(me.y + r + NX, NX) * COLS, COLS), COLS)

    jobs = {
        "m": [gather_z(me, tx, meta.at[me.ex], block_region(meta, 16))],
        "t": [gather_z(me, tx, tok_i, block_region(tok, BLOCK))],
        "g": [gather_xy(me, tx, own_half(gate_i, e), rows_region(e), e == 0) for e in (0, 1)],
        "u": [gather_xy(me, tx, own_half(up_i, e), rows_region(2 + e), e == 0) for e in (0, 1)],
        "d": [gather_xy(me, tx, own_half(down_i, e), cols_region(e), e == 0) for e in (0, 1)],
    }
    for i, r in enumerate(ROW_OF):
        jobs[str(i)] = [reduce_stripe(me, tx, i, stripe(r), tok, theirs, ring, big)]

    fsc, psc = fsc_i[...], psc_i[...]
    meta[me.ex] = jnp.concatenate([
        fid_i[...].astype(F32), pid_i[...].astype(F32),
        fsc / jnp.sum(fsc, axis=0, keepdims=True), psc / jnp.sum(psc, axis=0, keepdims=True)], axis=0)
    kept = {}

    def table_step():
        for cp in loads:
            cp.wait()
        bh, bl = split2(second[0])
        b3[0:RANK], b3[RANK:2 * RANK], b3[2 * RANK:] = bh, bh, bl
        (pa, wa), (pb, wb), (pp, wp) = tables(meta[...])
        turned = jnp.transpose(jnp.concatenate([pa, pb, pp, -wa, -wb, wp, pp, wp], axis=0))
        for q in range(QUADS):
            wt[q] = jnp.concatenate([
                put(RF, quad_col(turned, 0, q), quad_col(turned, 48, q)),
                put(RP, quad_col(turned, 32, q), quad_col(turned, 80, q)),
                put(RF, quad_col(turned, 16, q), quad_col(turned, 64, q)),
            ], axis=1).astype(BF)
        kept["rows"] = (pa, pb, pp)
        kept["share"] = wp
        kept["quad"] = iter(range(QUADS))
        kept["half"] = iter([(r, i) for r in ROW_OF for i in range(COLS // CHUNK)])
        kept["grad"] = iter(range(STRIPES))

    def gather_step():
        q = next(kept["quad"])
        pa, pb, pp = kept["rows"]
        oa, op, ob = pick(RF, quad_row(pa, q)), pick(RP, quad_row(pp, q)), pick(RF, quad_row(pb, q))
        sel[q] = op

        def body(i, _):
            at = pl.ds(pl.multiple_of(i * 512, 512), 512)
            t = tok[4 * q:4 * q + 4, :, at].reshape(TOKQ, 512)
            x0[q * RF:(q + 1) * RF, at] = dot(oa, t).astype(BF)
            x0[QUADS * RF + q * RP:QUADS * RF + (q + 1) * RP, at] = dot(op, t).astype(BF)
            x1[q * RF:(q + 1) * RF, at] = dot(ob, t).astype(BF)
            return 0

        lax.fori_loop(0, 4, body, 0)

    def product(x, e, m, first_row, parts, how, h=None):
        rows_m = x.shape[0] // m

        def body(i, _):
            lo = pl.multiple_of(lax.rem(i, m) * rows_m, rows_m)
            rr = pl.ds(lo, rows_m)
            ra_ = pl.ds(first_row + lo, rows_m)
            cc = pl.ds(pl.multiple_of(lax.div(i, m) * CHUNK, CHUNK), CHUNK)
            out = []
            for w in (0, 1):
                v = sum(dot(x[rr, stripe(r)], big[2 * w + e, stripe(r), cc]) for r in parts)
                out.append(v if how == "set" else acc[w, ra_, cc] + v)
            if how == "end":
                g, u = out
                h[rr, cc] = (g / (1.0 + jnp.exp(-g)) * u).astype(BF)
            else:
                acc[0, ra_, cc], acc[1, ra_, cc] = out
            return 0

        lax.fori_loop(0, m * (HIDDEN // CHUNK), body, 0)

    def row0_step():
        product(x0, 0, 2, 0, (0,), "set")
        product(x1, 1, 1, ROWS0, (0,), "set")

    def rows1_step():
        product(x0, 0, 2, 0, (-1, 1), "add")
        product(x1, 1, 1, ROWS0, (-1, 1), "add")

    def last0_step():
        product(x0, 0, 2, 0, (2,), "end", h0)

    def last1_step():
        product(x1, 1, 1, ROWS0, (2,), "end", h1)

    nt = (((1,), (1,)), ((), ()))
    tn = (((0,), (0,)), ((), ()))

    def low_step():
        tx.drain("mtgu")
        ah, al = split2(first[...])
        low2 = lax.dot_general(h0[QUADS * RF:, :], jnp.concatenate([ah, al], axis=0), nt, preferred_element_type=F32)
        low = low2[:, :RANK] + low2[:, RANK:]
        lh, ll = split2(low)
        low_s[...] = low
        low3[...] = jnp.concatenate([lh, ll, lh], axis=1)

    def spread_step():
        hid_t[...] = jnp.transpose(h0[QUADS * RF:, :])
        for q in range(QUADS):
            lq = low_s[q * RP:(q + 1) * RP, :]
            l1, l2 = split2(lq)
            l3 = (lq - l1.astype(F32) - l2.astype(F32)).astype(BF)
            s = lax.dot_general(jnp.concatenate([l1, l2, l3, jnp.zeros_like(l1)], axis=1), sel[q], tn,
                                preferred_element_type=F32)
            v = (s[0:RANK] + s[RANK:2 * RANK] + s[2 * RANK:3 * RANK]) * quad_row(kept["share"], q)
            hi, lo = split2(v)
            low_t[0:RANK, q * TOKQ:(q + 1) * TOKQ] = hi
            low_t[RANK:, q * TOKQ:(q + 1) * TOKQ] = lo

    def partial_step():
        r, i = next(kept["half"])
        at = pl.ds(pl.multiple_of(lax.rem(me.y + r + NX, NX) * COLS + i * CHUNK, CHUNK), CHUNK)

        def body(_, c):
            r0 = dot(h0[...], down[0, :, at])
            rp = r0[QUADS * RF:] + dot(low3[...], b3[:, at])
            r1 = dot(h1[...], down[1, :, at])
            for q in range(QUADS):
                rows[q, 0:RF] = r0[q * RF:(q + 1) * RF].astype(BF)
                rows[q, RF:RF + RP] = rp[q * RP:(q + 1) * RP].astype(BF)
                rows[q, RF + RP:] = r1[q * RF:(q + 1) * RF].astype(BF)
            for q in range(QUADS):
                tok[4 * q:4 * q + 4, :, at] = dot(wt[q], rows[q]).astype(BF).reshape(4, BLOCK, CHUNK)
            return c

        body(0, 0)

    got_b = {}

    def grad_step():
        i = next(kept["grad"])
        r = ROW_OF[i]
        res = big[i, :, 0:COLS]
        gb = dot(low_t[...], res)
        gbuf[i] = gb[:RANK] + gb[RANK:]
        tx.tag = "x"
        for dx in range(NX):
            if (dx, r) != (0, 0):
                block = lax.rem(me.x + dx, NX) * BLOCK
                got_b[dx, r] = tx.send(gbuf.at[i, :, pl.ds(pl.multiple_of(block, BLOCK), BLOCK)],
                                       rb.at[i * NX + dx], me.dev_xy(dx, r))
        v = lax.dot_general(b3[RANK:, stripe(r)], res, nt, preferred_element_type=F32)
        bt[...] = v if i == 0 else bt[...] + v

    steps = {"T": table_step, "Q": gather_step, "E": row0_step, "F": rows1_step, "L": last0_step, "l": last1_step,
             "W": low_step, "V": spread_step, "P": partial_step, "C": grad_step}
    for op in "".join(PLAN):
        if op in steps:
            steps[op]()
        else:
            tx.tag = op
            for j in jobs[op]:
                next(j)

    na = HIDDEN // GROUP
    for q in range(QUADS):
        at = slice(q * TOKQ, (q + 1) * TOKQ)
        v = (bt[:RANK, at] + bt[RANK:, at]) * quad_row(kept["share"], q)
        hi, lo = split2(v)
        picked = lax.dot_general(sel[q], jnp.concatenate([hi, lo], axis=0), nt, preferred_element_type=F32)
        back[q * RP:(q + 1) * RP, :] = picked.astype(BF)
    ga = dot(hid_t[...], back[...])
    gabuf[...] = ga[:, :RANK] + ga[:, RANK:]
    tx.tag = "x"
    got_a = {}
    for i, (dx, dy) in enumerate(peers):
        if (dx, dy) != (0, 0):
            lo = pl.multiple_of(me.xy(dx, dy) * na, na)
            got_a[dx, dy] = tx.send(gabuf.at[pl.ds(lo, na)], ra.at[i], me.dev_xy(dx, dy))
    tb = gbuf[0, :, pl.ds(pl.multiple_of(me.x * BLOCK, BLOCK), BLOCK)]
    for i, p in enumerate(peers):
        if p != (0, 0):
            tx.arrived(got_b[p], rb.at[i], me.dev_xy(*p))
            tb = tb + rb[i]
    gb_o[...] = tb
    ta = gabuf[pl.ds(pl.multiple_of(me.dp * na, na), na), :]
    for i, p in enumerate(peers):
        if p != (0, 0):
            tx.arrived(got_a[p], ra.at[i], me.dev_xy(*p))
            ta = ta + ra[i]
    ga_o[...] = ta
    assert tx.count == SENDS
    tx.drain("mtgud0123x")


def main_call(gate, up, down, tok, fid, pid, fsc, psc, first, second):
    sds = jax.ShapeDtypeStruct
    vm = pltpu.VMEM
    na, nb = HIDDEN // GROUP, WIDTH // GROUP
    return pl.pallas_call(
        main_kernel,
        out_shape=(sds((na, RANK), F32), sds((RANK, nb), F32)),
        in_specs=[ANY] * 4 + [VM] * 6,
        out_specs=(VM, VM),
        scratch_shapes=[
            vm((4, WIDTH, HIDDEN), BF), vm((2, HIDDEN, WIDTH), BF),
            vm((GROUP, BLOCK, WIDTH), BF), vm((GROUP, 16, BLOCK), F32),
            vm((ROWS0, WIDTH), BF), vm((ROWS1, WIDTH), BF), vm((2, ROWS0 + ROWS1, HIDDEN), F32),
            vm((ROWS0, HIDDEN), BF), vm((ROWS1, HIDDEN), BF),
            vm((QUADS, TOKQ, RQ), BF), vm((QUADS * RP, RANK), F32), vm((QUADS * RP, 3 * RANK), BF),
            vm((3 * RANK, WIDTH), BF), vm((QUADS, RQ, CHUNK), BF),
            vm((STRIPES, NZ, BLOCK, COLS), BF), vm((STRIPES, 14, BLOCK // 2, COLS), BF),
            vm((QUADS, RP, TOKQ), BF), vm((2 * RANK, GROUP * BLOCK), BF), vm((2 * RANK, GROUP * BLOCK), F32),
            vm((HIDDEN, QUADS * RP), BF), vm((QUADS * RP, 2 * RANK), BF), vm((STRIPES, RANK, COLS), F32),
            vm((HIDDEN, RANK), F32), vm((GROUP, na, RANK), F32), vm((GROUP, RANK, nb), F32),
            pltpu.SemaphoreType.DMA((SENDS,)), pltpu.SemaphoreType.DMA((SENDS,)), pltpu.SemaphoreType.DMA((4,)),
        ],
        compiler_params=pltpu.CompilerParams(collective_id=0, has_side_effects=True, vmem_limit_bytes=63 << 20),
        name="main",
    )(gate, up, down, tok, fid, pid, fsc, psc, first, second)


def shards(tokens, fid, pid, fsc, psc, gate, up, down, first, second):
    ga, gb = main_call(gate, up, down, tokens, fid.T, pid.T, fsc.T, psc.T, first[0].T, second)
    return ga[None], gb[None]


def solution(mesh):
    rows = P(("dp", "expert"), None)
    return jax.shard_map(
        shards,
        mesh=mesh,
        in_specs=(rows,) * 5 + (P("expert", "dp", None), P("expert", "dp", None), P("expert", None, "dp"),
                                P("expert", None, None), P("expert", None, None)),
        out_specs=(P("expert", "dp", None), P("expert", None, "dp")),
        check_vma=False,
    )
```

```python
import functools

import jax
import jax.numpy as jnp
from jax import lax
from jax.experimental import pallas as pl
from jax.experimental.pallas import tpu as pltpu
from jax.sharding import PartitionSpec as P

BF = jnp.bfloat16
F32 = jnp.float32
MESH = pl.DeviceIdType.MESH
ANY = pl.BlockSpec(memory_space=pl.ANY)
VM = pl.BlockSpec(memory_space=pltpu.VMEM)

NX = 4
NZ = 8
GROUP = 16
BLOCK = 128
WIDTH = 2048
HIDDEN = 768
RANK = 64
QUADS = 4
TOKQ = 4 * BLOCK
CAPF = 18
CAPP = 36
RF = 80
RP = 144
RQ = 2 * RF + RP
ROWS0 = QUADS * (RF + RP)
ROWS1 = QUADS * RF
CHUNK = 256


class Place:
    def __init__(self):
        dp, ex = lax.axis_index("dp"), lax.axis_index("expert")
        self.dp, self.ex = dp, ex
        self.x, self.y = lax.rem(dp, NX), lax.div(dp, NX)
        self.z, self.c = lax.div(ex, 2), lax.rem(ex, 2)

    def xy(self, dx, dy):
        return lax.rem(self.y + dy + NX, NX) * NX + lax.rem(self.x + dx + NX, NX)

    def zz(self, dz):
        return lax.rem(self.z + dz + NZ, NZ)

    def dev_xy(self, dx, dy):
        return (self.xy(dx, dy), self.ex)

    def dev_z(self, dz):
        return (self.dp, self.zz(dz) * 2 + self.c)

    def partner(self):
        return (self.dp, self.z * 2 + 1 - self.c)


def barrier(devices):
    sem = pltpu.get_barrier_semaphore()
    for d in devices:
        pl.semaphore_signal(sem, inc=1, device_id=d, device_id_type=MESH)
    pl.semaphore_wait(sem, len(devices))


class Sender:
    def __init__(self, send_sem, recv_sem):
        self.send_sem, self.recv_sem = send_sem, recv_sem
        self.count = 0
        self.sent = []
        self.tag = None

    def send(self, src, dst, device):
        n = self.count
        self.count += 1
        cp = pltpu.make_async_remote_copy(
            src_ref=src, dst_ref=dst, send_sem=self.send_sem.at[n], recv_sem=self.recv_sem.at[n],
            device_id=device, device_id_type=MESH,
        )
        cp.start()
        self.sent.append((self.tag, cp))
        return n

    def arrived(self, n, region, device):
        pltpu.make_async_remote_copy(
            src_ref=region, dst_ref=region, send_sem=self.send_sem.at[n], recv_sem=self.recv_sem.at[n],
            device_id=device, device_id_type=MESH,
        ).wait_recv()

    def drain(self, tags):
        for tag, cp in self.sent:
            if tag in tags:
                cp.wait_send()
        self.sent = [(tag, cp) for tag, cp in self.sent if tag not in tags]


def gather_z(me, tx, own, region):
    c = me.c
    plus = tx.send(own, region(me.z, c, None), me.dev_z(1))
    minus = tx.send(own, region(me.z, c, None), me.dev_z(-1))
    got = [(tx.send(own, region(me.z, c, None), me.partner()), 0, None)]
    yield
    for k in (1, 2, 3):
        zl, zr = me.zz(-k), me.zz(k)
        tx.arrived(plus, region(zl, c, None), me.dev_z(1))
        plus = (tx.send(region(zl, c, None), region(zl, c, None), me.dev_z(1)) if k < 3
                else tx.send(region(zl, c, 0), region(zl, c, 0), me.dev_z(1)))
        got.append((tx.send(region(zl, c, None), region(zl, c, None), me.partner()), -k, None))
        tx.arrived(minus, region(zr, c, None), me.dev_z(-1))
        minus = (tx.send(region(zr, c, None), region(zr, c, None), me.dev_z(-1)) if k < 3
                 else tx.send(region(zr, c, 1), region(zr, c, 1), me.dev_z(-1)))
        got.append((tx.send(region(zr, c, None), region(zr, c, None), me.partner()), k, None))
        yield
    zo = me.zz(4)
    tx.arrived(plus, region(zo, c, 0), me.dev_z(1))
    got.append((tx.send(region(zo, c, 0), region(zo, c, 0), me.partner()), 4, 0))
    tx.arrived(minus, region(zo, c, 1), me.dev_z(-1))
    got.append((tx.send(region(zo, c, 1), region(zo, c, 1), me.partner()), 4, 1))
    yield
    for n, k, h in got:
        tx.arrived(n, region(me.zz(k), 1 - c, h), me.partner())
    yield


def gather_xy(me, tx, own, region, x_first):
    def at(p, q):
        return (p, q) if x_first else (q, p)

    def reg(p, q, h, dp_=0, dq_=0):
        return region(*at(p, q), h, *at(dp_, dq_))

    def dev(p, q):
        return me.dev_xy(*at(p, q))

    def src(p, q, h):
        return own(h) if (p, q) == (0, 0) else reg(p, q, h)

    def ring(p, q, dp_, dq_):
        return (tx.send(src(p, q, None), reg(p, q, None, dp_, dq_), dev(dp_, dq_)),
                tx.send(src(p, q, None), reg(p, q, None, -dp_, -dq_), dev(-dp_, -dq_)))

    def relay(n, p, q, dp_, dq_, h):
        tx.arrived(n, reg(p, q, None), dev(dp_, dq_))
        return tx.send(reg(p, q, h), reg(p, q, h, dp_, dq_), dev(dp_, dq_))

    far = {}

    def along_q(p):
        a, b = second[p]
        far[p] = (relay(a, p, -1, 0, 1, 0), relay(b, p, 1, 0, -1, 1))

    def opposite(p):
        for h in (0, 1):
            tx.arrived(far[p][h], reg(p, 2, h), dev(0, 1))

    first = ring(0, 0, 1, 0)
    second = {0: ring(0, 0, 0, 1)}
    yield
    o0 = relay(first[0], -1, 0, 1, 0, 0)
    o1 = relay(first[1], 1, 0, -1, 0, 1)
    second[-1] = ring(-1, 0, 0, 1)
    second[1] = ring(1, 0, 0, 1)
    yield
    along_q(0)
    yield
    tx.arrived(o0, reg(2, 0, 0), dev(1, 0))
    tx.arrived(o1, reg(2, 0, 1), dev(-1, 0))
    second[2] = ring(2, 0, 0, 1)
    yield
    opposite(0)
    yield
    along_q(-1)
    along_q(1)
    yield
    along_q(2)
    yield
    opposite(-1)
    opposite(1)
    yield
    opposite(2)
    yield


def split2(v):
    hi = v.astype(BF)
    return hi, (v - hi.astype(F32)).astype(BF)


def dot(a, b):
    return jnp.dot(a, b, preferred_element_type=F32)


def tables(meta):
    ex = lax.axis_index("expert").astype(F32)
    row = lax.broadcasted_iota(jnp.int32, (BLOCK, BLOCK), 0)
    col = lax.broadcasted_iota(jnp.int32, (BLOCK, BLOCK), 1)
    before = (row < col).astype(BF)
    quarter = lax.rem(lax.broadcasted_iota(jnp.int32, (GROUP, BLOCK), 0), 4).astype(F32)

    def one(ids, shares, which, cap):
        hit = (ids == which).astype(F32)
        named = jnp.sum(hit, axis=1)
        share = jnp.sum(hit * shares, axis=1)
        pos = dot(named.astype(BF), before) + quarter * cap
        return jnp.where(named > 0, pos, -1.0), share

    fid, pid, fsh, psh = (meta[:, 4 * i:4 * i + 4, :] for i in range(4))
    a = one(fid, fsh, 2.0 * ex, CAPF)
    b = one(fid, fsh, 2.0 * ex + 1.0, CAPF)
    p = one(pid, psh, ex, CAPP)
    return a, b, p


def quad_row(v, q):
    return jnp.concatenate([v[4 * q + i:4 * q + i + 1, :] for i in range(4)], axis=1)


def quad_col(v, first, q):
    return jnp.concatenate([v[:, first + 4 * q + i:first + 4 * q + i + 1] for i in range(4)], axis=0)


def pick(rows, pos):
    slot = lax.broadcasted_iota(jnp.int32, (rows, TOKQ), 0).astype(F32)
    return (slot == pos).astype(BF)


def put(rows, pos, share):
    slot = lax.broadcasted_iota(jnp.int32, (TOKQ, rows), 1).astype(F32)
    return jnp.where(slot == pos, share, 0.0)


COLS = WIDTH // NX
NEAR = ((0, 0), (1, 0), (-1, 0), (0, 1), (0, -1), (2, 0), (0, 2), (1, 1), (1, -1), (-1, 1), (-1, -1),
        (2, 1), (2, -1), (1, 2), (-1, 2), (2, 2))
CUTS = (0, 1, 3, 5, 9, 13, 16)
STEPS_P = ((0, 1), (1, 3), (3, 5), (5, 7), (7, 9), (9, 11), (11, 13), (13, 15), (15, 16))
PARTS = ((0, 5), (5, 9), (9, 13), (13, 16))
STRIPES = len(CUTS) - 1
ORDER = (4, 3, -3, 2, -2, 1, -1, 0)
SENDS = 6 * 20 + 2 * 17 + STRIPES * (8 + 14 + 17) + 2 * (GROUP - 1)

PLAN = (
    "umtmgutgmutmgutgmugmTugtutQQQgdQEguFguLlWPd0dP101P201212012d",
    "0dP1d2P301d3P2d1Pd403P434P2505145315043024V253504352452314C5",
    "334C54C5C",
)


def reduce_stripe(me, tx, cols, part, theirs, ring, out):
    half = BLOCK // 2

    def mine(k, h=None):
        at = slice(None) if h is None else pl.ds(h * half, half)
        return part.at[me.zz(k) * 2 + me.c, at, cols]

    def region(z, c, h):
        lo = (z * 2 + c) * BLOCK
        if h is None:
            return out.at[pl.ds(pl.multiple_of(lo, BLOCK), BLOCK), :]
        return out.at[pl.ds(pl.multiple_of(lo + h * half, half), half), :]

    swap = {k: tx.send(part.at[me.zz(k) * 2 + 1 - me.c, :, cols], theirs.at[me.zz(k)], me.partner()) for k in ORDER}
    yield

    def pair_sum(k):
        tx.arrived(swap[k], theirs.at[me.zz(k)], me.partner())
        r = mine(k)
        r[...] = (r[...].astype(F32) + theirs[me.zz(k)].astype(F32)).astype(BF)

    slot, waiting = {}, {}

    def push(sign, h, j):
        r = mine(sign * j, h)
        if (sign, h) in waiting:
            n, s = waiting[(sign, h)]
            tx.arrived(n, ring.at[s], me.dev_z(sign))
            r[...] = (r[...].astype(F32) + ring[s].astype(F32)).astype(BF)
        s = slot.setdefault((sign, h, j), len(slot))
        waiting[(sign, h)] = (tx.send(r, ring.at[s], me.dev_z(sign)), s)

    pair_sum(4)
    push(1, 0, 4)
    push(-1, 1, 4)
    pair_sum(3)
    pair_sum(-3)
    push(1, 1, 3)
    push(-1, 0, 3)
    yield
    for j in (3, 2, 1):
        if j < 3:
            pair_sum(j)
            pair_sum(-j)
            push(1, 1, j)
            push(-1, 0, j)
        push(1, 0, j)
        push(-1, 1, j)
        yield
    pair_sum(0)
    for h in (1, 0):
        total = mine(0, h)[...].astype(F32)
        for sign in (1, -1):
            n, s = waiting[(sign, h)]
            tx.arrived(n, ring.at[s], me.dev_z(sign))
            total = total + ring[s].astype(F32)
        region(me.z, me.c, h)[...] = total.astype(BF)
    yield from gather_z(me, tx, region(me.z, me.c, None), region)


def main_kernel(gate_i, up_i, down_i, tok_i, fid_i, pid_i, fsc_i, psc_i, first, second, ga_o, gb_o,
                big, down, tok, meta, x0, x1, acc, h0, h1, wt, low_s, low3, b3, rows, theirs, ring,
                sel, low_t, bt, hid_t, back, gbuf, gabuf, ra, rb, send_sem, recv_sem, loc_sem):
    me = Place()
    tx = Sender(send_sem, recv_sem)
    mine = pl.ds(pl.multiple_of(me.dp * BLOCK, BLOCK), BLOCK)
    loads = [
        pltpu.make_async_copy(s, d, loc_sem.at[i]) for i, (s, d) in enumerate((
            (tok_i, tok.at[me.ex]), (gate_i, big.at[0:2, mine, :]),
            (up_i, big.at[2:4, mine, :]), (down_i, down.at[:, :, 0:BLOCK])))
    ]
    for cp in loads:
        cp.start()
    barrier([me.dev_xy(*p) for p in NEAR[1:]] + [me.dev_z(1), me.dev_z(-1), me.partner()])

    def block_region(ref, size):
        def region(z, c, h):
            v = ref.at[z * 2 + c]
            return v if h is None else v.at[pl.ds(h * (size // 2), size // 2)]
        return region

    def rows_region(i):
        def region(dx, dy, h, ex, ey):
            dp = me.xy(dx, dy)
            if h is None:
                return big.at[i, pl.ds(pl.multiple_of(dp * BLOCK, BLOCK), BLOCK), :]
            n = BLOCK // 2
            return big.at[i, pl.ds(pl.multiple_of(dp * BLOCK + h * n, n), n), :]
        return region

    def cols_region(e):
        def region(dx, dy, h, ex, ey):
            j = [(a % NX, b % NX) for a, b in NEAR].index(((dx - ex) % NX, (dy - ey) % NX))
            rows_h = slice(None) if h is None else pl.ds(h * (HIDDEN // 2), HIDDEN // 2)
            return down.at[e, rows_h, j * BLOCK:(j + 1) * BLOCK]
        return region

    def own_half(ref, e):
        def half(h):
            v = ref.at[e]
            n = v.shape[0] // 2
            return v if h is None else v.at[pl.ds(h * n, n)]
        return half

    def stripe(r):
        return pl.ds(pl.multiple_of(lax.rem(me.y + r + NX, NX) * COLS, COLS), COLS)

    jobs = {
        "m": [gather_z(me, tx, meta.at[me.ex], block_region(meta, 16))],
        "t": [gather_z(me, tx, tok_i, block_region(tok, BLOCK))],
        "g": [gather_xy(me, tx, own_half(gate_i, e), rows_region(e), e == 0) for e in (0, 1)],
        "u": [gather_xy(me, tx, own_half(up_i, e), rows_region(2 + e), e == 0) for e in (0, 1)],
        "d": [gather_xy(me, tx, own_half(down_i, e), cols_region(e), e == 0) for e in (0, 1)],
    }
    def span(lo, hi):
        return slice(lo * BLOCK, hi * BLOCK)

    for i in range(STRIPES):
        lo, hi = CUTS[i], CUTS[i + 1]
        home = [k for k, (a, b) in enumerate(PARTS) if a <= lo < b][0]
        base = PARTS[home][0]
        jobs[str(i)] = [reduce_stripe(me, tx, span(lo, hi), tok, theirs.at[:, :, span(lo, hi)], ring.at[:, :, span(lo, hi)],
                                      big.at[home, :, span(lo - base, hi - base)])]

    fsc, psc = fsc_i[...], psc_i[...]
    meta[me.ex] = jnp.concatenate([
        fid_i[...].astype(F32), pid_i[...].astype(F32),
        fsc / jnp.sum(fsc, axis=0, keepdims=True), psc / jnp.sum(psc, axis=0, keepdims=True)], axis=0)
    kept = {}

    def table_step():
        for cp in loads:
            cp.wait()
        for j, off in enumerate(NEAR):
            bh, bl = split2(second[0, :, pl.ds(pl.multiple_of(me.xy(*off) * BLOCK, BLOCK), BLOCK)])
            b3[:, span(j, j + 1)] = jnp.concatenate([bh, bh, bl], axis=0)
        (pa, wa), (pb, wb), (pp, wp) = tables(meta[...])
        turned = jnp.transpose(jnp.concatenate([pa, pb, pp, -wa, -wb, wp, pp, wp], axis=0))
        for q in range(QUADS):
            wt[q] = jnp.concatenate([
                put(RF, quad_col(turned, 0, q), quad_col(turned, 48, q)),
                put(RP, quad_col(turned, 32, q), quad_col(turned, 80, q)),
                put(RF, quad_col(turned, 16, q), quad_col(turned, 64, q)),
            ], axis=1).astype(BF)
        kept["rows"] = (pa, pb, pp)
        kept["share"] = wp
        kept["quad"] = iter(range(QUADS))
        kept["part"] = iter(STEPS_P)
        kept["grad"] = iter(range(len(PARTS)))

    def gather_step():
        q = next(kept["quad"])
        pa, pb, pp = kept["rows"]
        oa, op, ob = pick(RF, quad_row(pa, q)), pick(RP, quad_row(pp, q)), pick(RF, quad_row(pb, q))
        sel[q] = op

        def body(i, _):
            at = pl.ds(pl.multiple_of(i * 512, 512), 512)
            t = tok[4 * q:4 * q + 4, :, at].reshape(TOKQ, 512)
            x0[q * RF:(q + 1) * RF, at] = dot(oa, t).astype(BF)
            x0[QUADS * RF + q * RP:QUADS * RF + (q + 1) * RP, at] = dot(op, t).astype(BF)
            x1[q * RF:(q + 1) * RF, at] = dot(ob, t).astype(BF)
            return 0

        lax.fori_loop(0, 4, body, 0)

    def product(x, e, m, first_row, parts, how, h=None):
        rows_m = x.shape[0] // m

        def body(i, _):
            lo = pl.multiple_of(lax.rem(i, m) * rows_m, rows_m)
            rr = pl.ds(lo, rows_m)
            ra_ = pl.ds(first_row + lo, rows_m)
            cc = pl.ds(pl.multiple_of(lax.div(i, m) * CHUNK, CHUNK), CHUNK)
            out = []
            for w in (0, 1):
                v = sum(dot(x[rr, stripe(r)], big[2 * w + e, stripe(r), cc]) for r in parts)
                out.append(v if how == "set" else acc[w, ra_, cc] + v)
            if how == "end":
                g, u = out
                h[rr, cc] = (g / (1.0 + jnp.exp(-g)) * u).astype(BF)
            else:
                acc[0, ra_, cc], acc[1, ra_, cc] = out
            return 0

        lax.fori_loop(0, m * (HIDDEN // CHUNK), body, 0)

    def row0_step():
        product(x0, 0, 2, 0, (0,), "set")
        product(x1, 1, 1, ROWS0, (0,), "set")

    def rows1_step():
        product(x0, 0, 2, 0, (-1, 1), "add")
        product(x1, 1, 1, ROWS0, (-1, 1), "add")

    def last0_step():
        product(x0, 0, 2, 0, (2,), "end", h0)

    def last1_step():
        product(x1, 1, 1, ROWS0, (2,), "end", h1)

    nt = (((1,), (1,)), ((), ()))
    tn = (((0,), (0,)), ((), ()))

    def low_step():
        tx.drain("mtgu")
        ah, al = split2(first[...])
        low2 = lax.dot_general(h0[QUADS * RF:, :], jnp.concatenate([ah, al], axis=0), nt, preferred_element_type=F32)
        low = low2[:, :RANK] + low2[:, RANK:]
        lh, ll = split2(low)
        low_s[...] = low
        low3[...] = jnp.concatenate([lh, ll, lh], axis=1)

    def spread_step():
        hid_t[...] = jnp.transpose(h0[QUADS * RF:, :])
        for q in range(QUADS):
            lq = low_s[q * RP:(q + 1) * RP, :]
            l1, l2 = split2(lq)
            l3 = (lq - l1.astype(F32) - l2.astype(F32)).astype(BF)
            s = lax.dot_general(jnp.concatenate([l1, l2, l3, jnp.zeros_like(l1)], axis=1), sel[q], tn,
                                preferred_element_type=F32)
            v = (s[0:RANK] + s[RANK:2 * RANK] + s[2 * RANK:3 * RANK]) * quad_row(kept["share"], q)
            hi, lo = split2(v)
            low_t[0:RANK, q * TOKQ:(q + 1) * TOKQ] = hi
            low_t[RANK:, q * TOKQ:(q + 1) * TOKQ] = lo

    def partial_step():
        at = span(*next(kept["part"]))
        n = at.stop - at.start
        r0 = dot(h0[...], down[0, :, at])
        rp = r0[QUADS * RF:] + dot(low3[...], b3[:, at])
        r1 = dot(h1[...], down[1, :, at])
        for q in range(QUADS):
            rows[q, 0:RF, 0:n] = r0[q * RF:(q + 1) * RF].astype(BF)
            rows[q, RF:RF + RP, 0:n] = rp[q * RP:(q + 1) * RP].astype(BF)
            rows[q, RF + RP:, 0:n] = r1[q * RF:(q + 1) * RF].astype(BF)
        for q in range(QUADS):
            tok[4 * q:4 * q + 4, :, at] = dot(wt[q], rows[q, :, 0:n]).astype(BF).reshape(4, BLOCK, n)

    got_b = {}

    def grad_step():
        i = next(kept["grad"])
        lo, hi = PARTS[i]
        res = big[i, :, 0:(hi - lo) * BLOCK]
        gb = dot(low_t[...], res)
        gbuf[:, span(lo, hi)] = gb[:RANK] + gb[RANK:]
        tx.tag = "x"
        for j in range(max(lo, 1), hi):
            got_b[j] = tx.send(gbuf.at[:, span(j, j + 1)], rb.at[j], me.dev_xy(*NEAR[j]))
        v = lax.dot_general(b3[RANK:, span(lo, hi)], res, nt, preferred_element_type=F32)
        bt[...] = v if i == 0 else bt[...] + v

    steps = {"T": table_step, "Q": gather_step, "E": row0_step, "F": rows1_step, "L": last0_step, "l": last1_step,
             "W": low_step, "V": spread_step, "P": partial_step, "C": grad_step}
    for op in "".join(PLAN):
        if op in steps:
            steps[op]()
        else:
            tx.tag = op
            for j in jobs[op]:
                next(j)

    na = HIDDEN // GROUP
    for q in range(QUADS):
        at = slice(q * TOKQ, (q + 1) * TOKQ)
        v = (bt[:RANK, at] + bt[RANK:, at]) * quad_row(kept["share"], q)
        hi, lo = split2(v)
        picked = lax.dot_general(sel[q], jnp.concatenate([hi, lo], axis=0), nt, preferred_element_type=F32)
        back[q * RP:(q + 1) * RP, :] = picked.astype(BF)
    ga = dot(hid_t[...], back[...])
    gabuf[...] = ga[:, :RANK] + ga[:, RANK:]
    tx.tag = "x"
    got_a = {}
    for j in range(1, GROUP):
        lo = pl.multiple_of(me.xy(*NEAR[j]) * na, na)
        got_a[j] = tx.send(gabuf.at[pl.ds(lo, na)], ra.at[j], me.dev_xy(*NEAR[j]))
    tb = gbuf[:, 0:BLOCK]
    for j in range(1, GROUP):
        tx.arrived(got_b[j], rb.at[j], me.dev_xy(*NEAR[j]))
        tb = tb + rb[j]
    gb_o[...] = tb
    ta = gabuf[pl.ds(pl.multiple_of(me.dp * na, na), na), :]
    for j in range(1, GROUP):
        tx.arrived(got_a[j], ra.at[j], me.dev_xy(*NEAR[j]))
        ta = ta + ra[j]
    ga_o[...] = ta
    assert tx.count == SENDS
    tx.drain("mtgud012345x")


def main_call(gate, up, down, tok, fid, pid, fsc, psc, first, second):
    sds = jax.ShapeDtypeStruct
    vm = pltpu.VMEM
    na, nb = HIDDEN // GROUP, WIDTH // GROUP
    return pl.pallas_call(
        main_kernel,
        out_shape=(sds((na, RANK), F32), sds((RANK, nb), F32)),
        in_specs=[ANY] * 4 + [VM] * 6,
        out_specs=(VM, VM),
        scratch_shapes=[
            vm((4, WIDTH, HIDDEN), BF), vm((2, HIDDEN, WIDTH), BF),
            vm((GROUP, BLOCK, WIDTH), BF), vm((GROUP, 16, BLOCK), F32),
            vm((ROWS0, WIDTH), BF), vm((ROWS1, WIDTH), BF), vm((2, ROWS0 + ROWS1, HIDDEN), F32),
            vm((ROWS0, HIDDEN), BF), vm((ROWS1, HIDDEN), BF),
            vm((QUADS, TOKQ, RQ), BF), vm((QUADS * RP, RANK), F32), vm((QUADS * RP, 3 * RANK), BF),
            vm((3 * RANK, WIDTH), BF), vm((QUADS, RQ, CHUNK), BF),
            vm((NZ, BLOCK, WIDTH), BF), vm((14, BLOCK // 2, WIDTH), BF),
            vm((QUADS, RP, TOKQ), BF), vm((2 * RANK, GROUP * BLOCK), BF), vm((2 * RANK, GROUP * BLOCK), F32),
            vm((HIDDEN, QUADS * RP), BF), vm((QUADS * RP, 2 * RANK), BF), vm((RANK, WIDTH), F32),
            vm((HIDDEN, RANK), F32), vm((GROUP, na, RANK), F32), vm((GROUP, RANK, nb), F32),
            pltpu.SemaphoreType.DMA((SENDS,)), pltpu.SemaphoreType.DMA((SENDS,)), pltpu.SemaphoreType.DMA((4,)),
        ],
        compiler_params=pltpu.CompilerParams(collective_id=0, has_side_effects=True, vmem_limit_bytes=63 << 20),
        name="main",
    )(gate, up, down, tok, fid, pid, fsc, psc, first, second)


def shards(tokens, fid, pid, fsc, psc, gate, up, down, first, second):
    ga, gb = main_call(gate, up, down, tokens, fid.T, pid.T, fsc.T, psc.T, first[0].T, second)
    return ga[None], gb[None]


def solution(mesh):
    rows = P(("dp", "expert"), None)
    return jax.shard_map(
        shards,
        mesh=mesh,
        in_specs=(rows,) * 5 + (P("expert", "dp", None), P("expert", "dp", None), P("expert", None, "dp"),
                                P("expert", None, None), P("expert", None, None)),
        out_specs=(P("expert", "dp", None), P("expert", None, "dp")),
        check_vma=False,
    )
```

```python
import functools

import jax
import jax.numpy as jnp
from jax import lax
from jax.experimental import pallas as pl
from jax.experimental.pallas import tpu as pltpu
from jax.sharding import PartitionSpec as P

BF = jnp.bfloat16
F32 = jnp.float32
MESH = pl.DeviceIdType.MESH
ANY = pl.BlockSpec(memory_space=pl.ANY)
VM = pl.BlockSpec(memory_space=pltpu.VMEM)

NX = 4
NZ = 8
GROUP = 16
BLOCK = 128
WIDTH = 2048
HIDDEN = 768
RANK = 64
QUADS = 4
TOKQ = 4 * BLOCK
CAPF = 18
CAPP = 36
RF = 80
RP = 144
RQ = 2 * RF + RP
ROWS0 = QUADS * (RF + RP)
ROWS1 = QUADS * RF
CHUNK = 256


class Place:
    def __init__(self):
        dp, ex = lax.axis_index("dp"), lax.axis_index("expert")
        self.dp, self.ex = dp, ex
        self.x, self.y = lax.rem(dp, NX), lax.div(dp, NX)
        self.z, self.c = lax.div(ex, 2), lax.rem(ex, 2)

    def xy(self, dx, dy):
        return lax.rem(self.y + dy + NX, NX) * NX + lax.rem(self.x + dx + NX, NX)

    def zz(self, dz):
        return lax.rem(self.z + dz + NZ, NZ)

    def dev_xy(self, dx, dy):
        return (self.xy(dx, dy), self.ex)

    def dev_z(self, dz):
        return (self.dp, self.zz(dz) * 2 + self.c)

    def partner(self):
        return (self.dp, self.z * 2 + 1 - self.c)


def barrier(devices):
    sem = pltpu.get_barrier_semaphore()
    for d in devices:
        pl.semaphore_signal(sem, inc=1, device_id=d, device_id_type=MESH)
    pl.semaphore_wait(sem, len(devices))


class Sender:
    def __init__(self, send_sem, recv_sem):
        self.send_sem, self.recv_sem = send_sem, recv_sem
        self.count = 0
        self.sent = []
        self.tag = None

    def send(self, src, dst, device):
        n = self.count
        self.count += 1
        cp = pltpu.make_async_remote_copy(
            src_ref=src, dst_ref=dst, send_sem=self.send_sem.at[n], recv_sem=self.recv_sem.at[n],
            device_id=device, device_id_type=MESH,
        )
        cp.start()
        self.sent.append((self.tag, cp))
        return n

    def arrived(self, n, region, device):
        pltpu.make_async_remote_copy(
            src_ref=region, dst_ref=region, send_sem=self.send_sem.at[n], recv_sem=self.recv_sem.at[n],
            device_id=device, device_id_type=MESH,
        ).wait_recv()

    def drain(self, tags):
        for tag, cp in self.sent:
            if tag in tags:
                cp.wait_send()
        self.sent = [(tag, cp) for tag, cp in self.sent if tag not in tags]


def gather_z(me, tx, own, region):
    c = me.c
    plus = tx.send(own, region(me.z, c, None), me.dev_z(1))
    minus = tx.send(own, region(me.z, c, None), me.dev_z(-1))
    got = [(tx.send(own, region(me.z, c, None), me.partner()), 0, None)]
    yield
    for k in (1, 2, 3):
        zl, zr = me.zz(-k), me.zz(k)
        tx.arrived(plus, region(zl, c, None), me.dev_z(1))
        plus = (tx.send(region(zl, c, None), region(zl, c, None), me.dev_z(1)) if k < 3
                else tx.send(region(zl, c, 0), region(zl, c, 0), me.dev_z(1)))
        got.append((tx.send(region(zl, c, None), region(zl, c, None), me.partner()), -k, None))
        tx.arrived(minus, region(zr, c, None), me.dev_z(-1))
        minus = (tx.send(region(zr, c, None), region(zr, c, None), me.dev_z(-1)) if k < 3
                 else tx.send(region(zr, c, 1), region(zr, c, 1), me.dev_z(-1)))
        got.append((tx.send(region(zr, c, None), region(zr, c, None), me.partner()), k, None))
        yield
    zo = me.zz(4)
    tx.arrived(plus, region(zo, c, 0), me.dev_z(1))
    got.append((tx.send(region(zo, c, 0), region(zo, c, 0), me.partner()), 4, 0))
    tx.arrived(minus, region(zo, c, 1), me.dev_z(-1))
    got.append((tx.send(region(zo, c, 1), region(zo, c, 1), me.partner()), 4, 1))
    yield
    for n, k, h in got:
        tx.arrived(n, region(me.zz(k), 1 - c, h), me.partner())
    yield


def gather_xy(me, tx, own, region, x_first):
    def at(p, q):
        return (p, q) if x_first else (q, p)

    def reg(p, q, h, dp_=0, dq_=0):
        return region(*at(p, q), h, *at(dp_, dq_))

    def dev(p, q):
        return me.dev_xy(*at(p, q))

    def src(p, q, h):
        return own(h) if (p, q) == (0, 0) else reg(p, q, h)

    def ring(p, q, dp_, dq_):
        return (tx.send(src(p, q, None), reg(p, q, None, dp_, dq_), dev(dp_, dq_)),
                tx.send(src(p, q, None), reg(p, q, None, -dp_, -dq_), dev(-dp_, -dq_)))

    def relay(n, p, q, dp_, dq_, h):
        tx.arrived(n, reg(p, q, None), dev(dp_, dq_))
        return tx.send(reg(p, q, h), reg(p, q, h, dp_, dq_), dev(dp_, dq_))

    far = {}

    def along_q(p):
        a, b = second[p]
        far[p] = (relay(a, p, -1, 0, 1, 0), relay(b, p, 1, 0, -1, 1))

    def opposite(p):
        for h in (0, 1):
            tx.arrived(far[p][h], reg(p, 2, h), dev(0, 1))

    first = ring(0, 0, 1, 0)
    second = {0: ring(0, 0, 0, 1)}
    yield
    o0 = relay(first[0], -1, 0, 1, 0, 0)
    o1 = relay(first[1], 1, 0, -1, 0, 1)
    second[-1] = ring(-1, 0, 0, 1)
    second[1] = ring(1, 0, 0, 1)
    yield
    along_q(0)
    yield
    tx.arrived(o0, reg(2, 0, 0), dev(1, 0))
    tx.arrived(o1, reg(2, 0, 1), dev(-1, 0))
    second[2] = ring(2, 0, 0, 1)
    yield
    opposite(0)
    yield
    along_q(-1)
    along_q(1)
    yield
    along_q(2)
    yield
    opposite(-1)
    opposite(1)
    yield
    opposite(2)
    yield


def split2(v):
    hi = v.astype(BF)
    return hi, (v - hi.astype(F32)).astype(BF)


def dot(a, b):
    return jnp.dot(a, b, preferred_element_type=F32)


def tables(meta):
    ex = lax.axis_index("expert").astype(F32)
    row = lax.broadcasted_iota(jnp.int32, (BLOCK, BLOCK), 0)
    col = lax.broadcasted_iota(jnp.int32, (BLOCK, BLOCK), 1)
    before = (row < col).astype(BF)
    quarter = lax.rem(lax.broadcasted_iota(jnp.int32, (GROUP, BLOCK), 0), 4).astype(F32)

    def one(ids, shares, which, cap):
        hit = (ids == which).astype(F32)
        named = jnp.sum(hit, axis=1)
        share = jnp.sum(hit * shares, axis=1)
        pos = dot(named.astype(BF), before) + quarter * cap
        return jnp.where(named > 0, pos, -1.0), share

    fid, pid, fsh, psh = (meta[:, 4 * i:4 * i + 4, :] for i in range(4))
    a = one(fid, fsh, 2.0 * ex, CAPF)
    b = one(fid, fsh, 2.0 * ex + 1.0, CAPF)
    p = one(pid, psh, ex, CAPP)
    return a, b, p


def quad_row(v, q):
    return jnp.concatenate([v[4 * q + i:4 * q + i + 1, :] for i in range(4)], axis=1)


def quad_col(v, first, q):
    return jnp.concatenate([v[:, first + 4 * q + i:first + 4 * q + i + 1] for i in range(4)], axis=0)


def pick(rows, pos):
    slot = lax.broadcasted_iota(jnp.int32, (rows, TOKQ), 0).astype(F32)
    return (slot == pos).astype(BF)


def put(rows, pos, share):
    slot = lax.broadcasted_iota(jnp.int32, (TOKQ, rows), 1).astype(F32)
    return jnp.where(slot == pos, share, 0.0)


COLS = WIDTH // NX
NEAR = ((0, 0), (1, 0), (-1, 0), (0, 1), (0, -1), (2, 0), (0, 2), (1, 1), (1, -1), (-1, 1), (-1, -1),
        (2, 1), (2, -1), (1, 2), (-1, 2), (2, 2))
CUTS = (0, 1, 3, 5, 9, 13, 16)
STEPS_P = ((0, 1), (1, 3), (3, 5), (5, 7), (7, 9), (9, 11), (11, 13), (13, 15), (15, 16))
PARTS = ((0, 5), (5, 9), (9, 13), (13, 16))
STRIPES = len(CUTS) - 1
ORDER = (4, 3, -3, 2, -2, 1, -1, 0)
SENDS = 6 * 20 + 2 * 17 + STRIPES * (8 + 14 + 17) + 2 * (GROUP - 1)

PLAN = (
    "gmtmuggtuumtmtggugmmuTugttQQQQEueudgFgfuGLlWP00ddP101P021210",
    "210d2dP01d2P0313Pd1d2P34421d3P4P552051405354523V52434034215C",
    "345334C54C5C",
)


def reduce_stripe(me, tx, cols, part, theirs, ring, out):
    half = BLOCK // 2

    def mine(k, h=None):
        at = slice(None) if h is None else pl.ds(h * half, half)
        return part.at[me.zz(k) * 2 + me.c, at, cols]

    def region(z, c, h):
        lo = (z * 2 + c) * BLOCK
        if h is None:
            return out.at[pl.ds(pl.multiple_of(lo, BLOCK), BLOCK), :]
        return out.at[pl.ds(pl.multiple_of(lo + h * half, half), half), :]

    swap = {k: tx.send(part.at[me.zz(k) * 2 + 1 - me.c, :, cols], theirs.at[me.zz(k)], me.partner()) for k in ORDER}
    yield

    def pair_sum(k):
        tx.arrived(swap[k], theirs.at[me.zz(k)], me.partner())
        r = mine(k)
        r[...] = (r[...].astype(F32) + theirs[me.zz(k)].astype(F32)).astype(BF)

    slot, waiting = {}, {}

    def push(sign, h, j):
        r = mine(sign * j, h)
        if (sign, h) in waiting:
            n, s = waiting[(sign, h)]
            tx.arrived(n, ring.at[s], me.dev_z(sign))
            r[...] = (r[...].astype(F32) + ring[s].astype(F32)).astype(BF)
        s = slot.setdefault((sign, h, j), len(slot))
        waiting[(sign, h)] = (tx.send(r, ring.at[s], me.dev_z(sign)), s)

    pair_sum(4)
    push(1, 0, 4)
    push(-1, 1, 4)
    pair_sum(3)
    pair_sum(-3)
    push(1, 1, 3)
    push(-1, 0, 3)
    yield
    for j in (3, 2, 1):
        if j < 3:
            pair_sum(j)
            pair_sum(-j)
            push(1, 1, j)
            push(-1, 0, j)
        push(1, 0, j)
        push(-1, 1, j)
        yield
    pair_sum(0)
    for h in (1, 0):
        total = mine(0, h)[...].astype(F32)
        for sign in (1, -1):
            n, s = waiting[(sign, h)]
            tx.arrived(n, ring.at[s], me.dev_z(sign))
            total = total + ring[s].astype(F32)
        region(me.z, me.c, h)[...] = total.astype(BF)
    yield from gather_z(me, tx, region(me.z, me.c, None), region)


def main_kernel(gate_i, up_i, down_i, tok_i, fid_i, pid_i, fsc_i, psc_i, first, second, ga_o, gb_o,
                big, down, tok, meta, x0, x1, acc, h0, h1, wt, low_s, low3, b3, rows, theirs, ring,
                sel, low_t, bt, hid_t, back, gbuf, gabuf, ra, rb, send_sem, recv_sem, loc_sem):
    me = Place()
    tx = Sender(send_sem, recv_sem)
    mine = pl.ds(pl.multiple_of(me.dp * BLOCK, BLOCK), BLOCK)
    loads = [
        pltpu.make_async_copy(s, d, loc_sem.at[i]) for i, (s, d) in enumerate((
            (tok_i, tok.at[me.ex]), (gate_i, big.at[0:2, mine, :]),
            (up_i, big.at[2:4, mine, :]), (down_i, down.at[:, :, 0:BLOCK])))
    ]
    for cp in loads:
        cp.start()
    fsc, psc = fsc_i[...], psc_i[...]
    meta[me.ex] = jnp.concatenate([
        fid_i[...].astype(F32), pid_i[...].astype(F32),
        fsc / jnp.sum(fsc, axis=0, keepdims=True), psc / jnp.sum(psc, axis=0, keepdims=True)], axis=0)
    barrier([me.dev_xy(*p) for p in NEAR[1:]] + [me.dev_z(1), me.dev_z(-1), me.partner()])

    def block_region(ref, size):
        def region(z, c, h):
            v = ref.at[z * 2 + c]
            return v if h is None else v.at[pl.ds(h * (size // 2), size // 2)]
        return region

    def rows_region(i):
        def region(dx, dy, h, ex, ey):
            dp = me.xy(dx, dy)
            if h is None:
                return big.at[i, pl.ds(pl.multiple_of(dp * BLOCK, BLOCK), BLOCK), :]
            n = BLOCK // 2
            return big.at[i, pl.ds(pl.multiple_of(dp * BLOCK + h * n, n), n), :]
        return region

    def cols_region(e):
        def region(dx, dy, h, ex, ey):
            j = [(a % NX, b % NX) for a, b in NEAR].index(((dx - ex) % NX, (dy - ey) % NX))
            rows_h = slice(None) if h is None else pl.ds(h * (HIDDEN // 2), HIDDEN // 2)
            return down.at[e, rows_h, j * BLOCK:(j + 1) * BLOCK]
        return region

    def own_half(ref, e):
        def half(h):
            v = ref.at[e]
            n = v.shape[0] // 2
            return v if h is None else v.at[pl.ds(h * n, n)]
        return half

    def stripe(r):
        return pl.ds(pl.multiple_of(lax.rem(me.y + r + NX, NX) * COLS, COLS), COLS)

    jobs = {
        "m": [gather_z(me, tx, meta.at[me.ex], block_region(meta, 16))],
        "t": [gather_z(me, tx, tok_i, block_region(tok, BLOCK))],
        "g": [gather_xy(me, tx, own_half(gate_i, e), rows_region(e), e == 0) for e in (0, 1)],
        "u": [gather_xy(me, tx, own_half(up_i, e), rows_region(2 + e), e == 0) for e in (0, 1)],
        "d": [gather_xy(me, tx, own_half(down_i, e), cols_region(e), e == 0) for e in (0, 1)],
    }
    def span(lo, hi):
        return slice(lo * BLOCK, hi * BLOCK)

    for i in range(STRIPES):
        lo, hi = CUTS[i], CUTS[i + 1]
        home = [k for k, (a, b) in enumerate(PARTS) if a <= lo < b][0]
        base = PARTS[home][0]
        jobs[str(i)] = [reduce_stripe(me, tx, span(lo, hi), tok, theirs.at[:, :, span(lo, hi)], ring.at[:, :, span(lo, hi)],
                                      big.at[home, :, span(lo - base, hi - base)])]

    kept = {}

    def table_step():
        for cp in loads:
            cp.wait()
        for j, off in enumerate(NEAR):
            bh, bl = split2(second[0, :, pl.ds(pl.multiple_of(me.xy(*off) * BLOCK, BLOCK), BLOCK)])
            b3[:, span(j, j + 1)] = jnp.concatenate([bh, bh, bl], axis=0)
        (pa, wa), (pb, wb), (pp, wp) = tables(meta[...])
        turned = jnp.transpose(jnp.concatenate([pa, pb, pp, -wa, -wb, wp, pp, wp], axis=0))
        for q in range(QUADS):
            wt[q] = jnp.concatenate([
                put(RF, quad_col(turned, 0, q), quad_col(turned, 48, q)),
                put(RP, quad_col(turned, 32, q), quad_col(turned, 80, q)),
                put(RF, quad_col(turned, 16, q), quad_col(turned, 64, q)),
            ], axis=1).astype(BF)
        kept["rows"] = (pa, pb, pp)
        kept["share"] = wp
        kept["quad"] = iter(range(QUADS))
        kept["part"] = iter(STEPS_P)
        kept["grad"] = iter(range(len(PARTS)))

    def gather_step():
        q = next(kept["quad"])
        pa, pb, pp = kept["rows"]
        oa, op, ob = pick(RF, quad_row(pa, q)), pick(RP, quad_row(pp, q)), pick(RF, quad_row(pb, q))
        sel[q] = op

        def body(i, _):
            at = pl.ds(pl.multiple_of(i * 512, 512), 512)
            t = tok[4 * q:4 * q + 4, :, at].reshape(TOKQ, 512)
            x0[q * RF:(q + 1) * RF, at] = dot(oa, t).astype(BF)
            x0[QUADS * RF + q * RP:QUADS * RF + (q + 1) * RP, at] = dot(op, t).astype(BF)
            x1[q * RF:(q + 1) * RF, at] = dot(ob, t).astype(BF)
            return 0

        lax.fori_loop(0, 4, body, 0)

    def product(x, e, m, first_row, w, parts, h=None):
        rows_m = x.shape[0] // m

        def body(i, _):
            lo = pl.multiple_of(lax.rem(i, m) * rows_m, rows_m)
            rr = pl.ds(lo, rows_m)
            ra_ = pl.ds(first_row + lo, rows_m)
            cc = pl.ds(pl.multiple_of(lax.div(i, m) * CHUNK, CHUNK), CHUNK)
            v = sum(dot(x[rr, stripe(r)], big[2 * w + e, stripe(r), cc]) for r in parts)
            if parts != (0,):
                v = acc[w, ra_, cc] + v
            if h is None:
                acc[w, ra_, cc] = v
            else:
                g = acc[0, ra_, cc]
                h[rr, cc] = (g / (1.0 + jnp.exp(-g)) * v).astype(BF)
            return 0

        lax.fori_loop(0, m * (HIDDEN // CHUNK), body, 0)

    def both(w, parts):
        def step_of():
            product(x0, 0, 2, 0, w, parts)
            product(x1, 1, 1, ROWS0, w, parts)
        return step_of

    def last0_step():
        product(x0, 0, 2, 0, 1, (2,), h0)

    def last1_step():
        product(x1, 1, 1, ROWS0, 1, (2,), h1)

    nt = (((1,), (1,)), ((), ()))
    tn = (((0,), (0,)), ((), ()))

    def low_step():
        tx.drain("mtgu")
        ah, al = split2(first[...])
        low2 = lax.dot_general(h0[QUADS * RF:, :], jnp.concatenate([ah, al], axis=0), nt, preferred_element_type=F32)
        low = low2[:, :RANK] + low2[:, RANK:]
        lh, ll = split2(low)
        low_s[...] = low
        low3[...] = jnp.concatenate([lh, ll, lh], axis=1)

    def spread_step():
        hid_t[...] = jnp.transpose(h0[QUADS * RF:, :])
        for q in range(QUADS):
            lq = low_s[q * RP:(q + 1) * RP, :]
            l1, l2 = split2(lq)
            l3 = (lq - l1.astype(F32) - l2.astype(F32)).astype(BF)
            s = lax.dot_general(jnp.concatenate([l1, l2, l3, jnp.zeros_like(l1)], axis=1), sel[q], tn,
                                preferred_element_type=F32)
            v = (s[0:RANK] + s[RANK:2 * RANK] + s[2 * RANK:3 * RANK]) * quad_row(kept["share"], q)
            hi, lo = split2(v)
            low_t[0:RANK, q * TOKQ:(q + 1) * TOKQ] = hi
            low_t[RANK:, q * TOKQ:(q + 1) * TOKQ] = lo

    def partial_step():
        at = span(*next(kept["part"]))
        n = at.stop - at.start
        r0 = dot(h0[...], down[0, :, at])
        rp = r0[QUADS * RF:] + dot(low3[...], b3[:, at])
        r1 = dot(h1[...], down[1, :, at])
        for q in range(QUADS):
            rows[q, 0:RF, 0:n] = r0[q * RF:(q + 1) * RF].astype(BF)
            rows[q, RF:RF + RP, 0:n] = rp[q * RP:(q + 1) * RP].astype(BF)
            rows[q, RF + RP:, 0:n] = r1[q * RF:(q + 1) * RF].astype(BF)
        for q in range(QUADS):
            tok[4 * q:4 * q + 4, :, at] = dot(wt[q], rows[q, :, 0:n]).astype(BF).reshape(4, BLOCK, n)

    got_b = {}

    def grad_b(i):
        lo, hi = PARTS[i]
        gb = dot(low_t[...], big[i, :, 0:(hi - lo) * BLOCK])
        gbuf[:, span(lo, hi)] = gb[:RANK] + gb[RANK:]
        tx.tag = "x"
        for j in reversed(range(max(lo, 1), hi)):
            got_b[j] = tx.send(gbuf.at[:, span(j, j + 1)], rb.at[j], me.dev_xy(*NEAR[j]))

    def grad_step():
        i = next(kept["grad"])
        lo, hi = PARTS[i]
        v = lax.dot_general(b3[RANK:, span(lo, hi)], big[i, :, 0:(hi - lo) * BLOCK], nt, preferred_element_type=F32)
        bt[...] = v if i == 0 else bt[...] + v
        if i < len(PARTS) - 1:
            grad_b(i)

    steps = {"T": table_step, "Q": gather_step, "E": both(0, (0,)), "e": both(1, (0,)), "F": both(0, (-1, 1)),
             "f": both(1, (-1, 1)), "G": both(0, (2,)), "L": last0_step, "l": last1_step,
             "W": low_step, "V": spread_step, "P": partial_step, "C": grad_step}
    for op in "".join(PLAN):
        if op in steps:
            steps[op]()
        else:
            tx.tag = op
            for j in jobs[op]:
                next(j)

    na = HIDDEN // GROUP
    for q in range(QUADS):
        at = slice(q * TOKQ, (q + 1) * TOKQ)
        v = (bt[:RANK, at] + bt[RANK:, at]) * quad_row(kept["share"], q)
        hi, lo = split2(v)
        picked = lax.dot_general(sel[q], jnp.concatenate([hi, lo], axis=0), nt, preferred_element_type=F32)
        back[q * RP:(q + 1) * RP, :] = picked.astype(BF)
    ga = dot(hid_t[...], back[...])
    gabuf[...] = ga[:, :RANK] + ga[:, RANK:]
    tx.tag = "x"
    got_a = {}
    for j in reversed(range(1, GROUP)):
        lo = pl.multiple_of(me.xy(*NEAR[j]) * na, na)
        got_a[j] = tx.send(gabuf.at[pl.ds(lo, na)], ra.at[j], me.dev_xy(*NEAR[j]))
    grad_b(len(PARTS) - 1)
    tb = gbuf[:, 0:BLOCK]
    for j in range(1, GROUP):
        tx.arrived(got_b[j], rb.at[j], me.dev_xy(*NEAR[j]))
        tb = tb + rb[j]
    gb_o[...] = tb
    ta = gabuf[pl.ds(pl.multiple_of(me.dp * na, na), na), :]
    for j in range(1, GROUP):
        tx.arrived(got_a[j], ra.at[j], me.dev_xy(*NEAR[j]))
        ta = ta + ra[j]
    ga_o[...] = ta
    assert tx.count == SENDS
    tx.drain("mtgud012345x")


def main_call(gate, up, down, tok, fid, pid, fsc, psc, first, second):
    sds = jax.ShapeDtypeStruct
    vm = pltpu.VMEM
    na, nb = HIDDEN // GROUP, WIDTH // GROUP
    return pl.pallas_call(
        main_kernel,
        out_shape=(sds((na, RANK), F32), sds((RANK, nb), F32)),
        in_specs=[ANY] * 4 + [VM] * 6,
        out_specs=(VM, VM),
        scratch_shapes=[
            vm((4, WIDTH, HIDDEN), BF), vm((2, HIDDEN, WIDTH), BF),
            vm((GROUP, BLOCK, WIDTH), BF), vm((GROUP, 16, BLOCK), F32),
            vm((ROWS0, WIDTH), BF), vm((ROWS1, WIDTH), BF), vm((2, ROWS0 + ROWS1, HIDDEN), F32),
            vm((ROWS0, HIDDEN), BF), vm((ROWS1, HIDDEN), BF),
            vm((QUADS, TOKQ, RQ), BF), vm((QUADS * RP, RANK), F32), vm((QUADS * RP, 3 * RANK), BF),
            vm((3 * RANK, WIDTH), BF), vm((QUADS, RQ, CHUNK), BF),
            vm((NZ, BLOCK, WIDTH), BF), vm((14, BLOCK // 2, WIDTH), BF),
            vm((QUADS, RP, TOKQ), BF), vm((2 * RANK, GROUP * BLOCK), BF), vm((2 * RANK, GROUP * BLOCK), F32),
            vm((HIDDEN, QUADS * RP), BF), vm((QUADS * RP, 2 * RANK), BF), vm((RANK, WIDTH), F32),
            vm((HIDDEN, RANK), F32), vm((GROUP, na, RANK), F32), vm((GROUP, RANK, nb), F32),
            pltpu.SemaphoreType.DMA((SENDS,)), pltpu.SemaphoreType.DMA((SENDS,)), pltpu.SemaphoreType.DMA((4,)),
        ],
        compiler_params=pltpu.CompilerParams(collective_id=0, has_side_effects=True, vmem_limit_bytes=63 << 20),
        name="main",
    )(gate, up, down, tok, fid, pid, fsc, psc, first, second)


def shards(tokens, fid, pid, fsc, psc, gate, up, down, first, second):
    ga, gb = main_call(gate, up, down, tokens, fid.T, pid.T, fsc.T, psc.T, first[0].T, second)
    return ga[None], gb[None]


def solution(mesh):
    rows = P(("dp", "expert"), None)
    return jax.shard_map(
        shards,
        mesh=mesh,
        in_specs=(rows,) * 5 + (P("expert", "dp", None), P("expert", "dp", None), P("expert", None, "dp"),
                                P("expert", None, None), P("expert", None, None)),
        out_specs=(P("expert", "dp", None), P("expert", None, "dp")),
        check_vma=False,
    )
```

```python
import functools

import jax
import jax.numpy as jnp
from jax import lax
from jax.experimental import pallas as pl
from jax.experimental.pallas import tpu as pltpu
from jax.sharding import PartitionSpec as P

BF = jnp.bfloat16
F32 = jnp.float32
MESH = pl.DeviceIdType.MESH
ANY = pl.BlockSpec(memory_space=pl.ANY)
VM = pl.BlockSpec(memory_space=pltpu.VMEM)

NX = 4
NZ = 8
GROUP = 16
BLOCK = 128
WIDTH = 2048
HIDDEN = 768
RANK = 64
QUADS = 4
TOKQ = 4 * BLOCK
CAPF = 18
CAPP = 36
RF = 80
RP = 144
RQ = 2 * RF + RP
ROWS0 = QUADS * (RF + RP)
ROWS1 = QUADS * RF
CHUNK = 256


class Place:
    def __init__(self):
        dp, ex = lax.axis_index("dp"), lax.axis_index("expert")
        self.dp, self.ex = dp, ex
        self.x, self.y = lax.rem(dp, NX), lax.div(dp, NX)
        self.z, self.c = lax.div(ex, 2), lax.rem(ex, 2)

    def xy(self, dx, dy):
        return lax.rem(self.y + dy + NX, NX) * NX + lax.rem(self.x + dx + NX, NX)

    def zz(self, dz):
        return lax.rem(self.z + dz + NZ, NZ)

    def dev_xy(self, dx, dy):
        return (self.xy(dx, dy), self.ex)

    def dev_z(self, dz):
        return (self.dp, self.zz(dz) * 2 + self.c)

    def partner(self):
        return (self.dp, self.z * 2 + 1 - self.c)


def barrier(devices):
    sem = pltpu.get_barrier_semaphore()
    for d in devices:
        pl.semaphore_signal(sem, inc=1, device_id=d, device_id_type=MESH)
    pl.semaphore_wait(sem, len(devices))


class Sender:
    def __init__(self, send_sem, recv_sem):
        self.send_sem, self.recv_sem = send_sem, recv_sem
        self.count = 0
        self.sent = []
        self.tag = None

    def send(self, src, dst, device):
        n = self.count
        self.count += 1
        cp = pltpu.make_async_remote_copy(
            src_ref=src, dst_ref=dst, send_sem=self.send_sem.at[n], recv_sem=self.recv_sem.at[n],
            device_id=device, device_id_type=MESH,
        )
        cp.start()
        self.sent.append((self.tag, cp))
        return n

    def arrived(self, n, region, device):
        pltpu.make_async_remote_copy(
            src_ref=region, dst_ref=region, send_sem=self.send_sem.at[n], recv_sem=self.recv_sem.at[n],
            device_id=device, device_id_type=MESH,
        ).wait_recv()

    def drain(self, tags):
        for tag, cp in self.sent:
            if tag in tags:
                cp.wait_send()
        self.sent = [(tag, cp) for tag, cp in self.sent if tag not in tags]


def gather_z(me, tx, own, region):
    c = me.c
    plus = tx.send(own, region(me.z, c, None), me.dev_z(1))
    minus = tx.send(own, region(me.z, c, None), me.dev_z(-1))
    got = [(tx.send(own, region(me.z, c, None), me.partner()), 0, None)]
    yield
    for k in (1, 2, 3):
        zl, zr = me.zz(-k), me.zz(k)
        tx.arrived(plus, region(zl, c, None), me.dev_z(1))
        plus = (tx.send(region(zl, c, None), region(zl, c, None), me.dev_z(1)) if k < 3
                else tx.send(region(zl, c, 0), region(zl, c, 0), me.dev_z(1)))
        got.append((tx.send(region(zl, c, None), region(zl, c, None), me.partner()), -k, None))
        tx.arrived(minus, region(zr, c, None), me.dev_z(-1))
        minus = (tx.send(region(zr, c, None), region(zr, c, None), me.dev_z(-1)) if k < 3
                 else tx.send(region(zr, c, 1), region(zr, c, 1), me.dev_z(-1)))
        got.append((tx.send(region(zr, c, None), region(zr, c, None), me.partner()), k, None))
        yield
    zo = me.zz(4)
    tx.arrived(plus, region(zo, c, 0), me.dev_z(1))
    got.append((tx.send(region(zo, c, 0), region(zo, c, 0), me.partner()), 4, 0))
    tx.arrived(minus, region(zo, c, 1), me.dev_z(-1))
    got.append((tx.send(region(zo, c, 1), region(zo, c, 1), me.partner()), 4, 1))
    yield
    for n, k, h in got:
        tx.arrived(n, region(me.zz(k), 1 - c, h), me.partner())
    yield


def gather_xy(me, tx, own, region, x_first):
    def at(p, q):
        return (p, q) if x_first else (q, p)

    def reg(p, q, h, dp_=0, dq_=0):
        return region(*at(p, q), h, *at(dp_, dq_))

    def dev(p, q):
        return me.dev_xy(*at(p, q))

    def src(p, q, h):
        return own(h) if (p, q) == (0, 0) else reg(p, q, h)

    def ring(p, q, dp_, dq_):
        return (tx.send(src(p, q, None), reg(p, q, None, dp_, dq_), dev(dp_, dq_)),
                tx.send(src(p, q, None), reg(p, q, None, -dp_, -dq_), dev(-dp_, -dq_)))

    def relay(n, p, q, dp_, dq_, h):
        tx.arrived(n, reg(p, q, None), dev(dp_, dq_))
        return tx.send(reg(p, q, h), reg(p, q, h, dp_, dq_), dev(dp_, dq_))

    far = {}

    def along_q(p):
        a, b = second[p]
        far[p] = (relay(a, p, -1, 0, 1, 0), relay(b, p, 1, 0, -1, 1))

    def opposite(p):
        for h in (0, 1):
            tx.arrived(far[p][h], reg(p, 2, h), dev(0, 1))

    first = ring(0, 0, 1, 0)
    second = {0: ring(0, 0, 0, 1)}
    yield
    o0 = relay(first[0], -1, 0, 1, 0, 0)
    o1 = relay(first[1], 1, 0, -1, 0, 1)
    second[-1] = ring(-1, 0, 0, 1)
    second[1] = ring(1, 0, 0, 1)
    yield
    along_q(0)
    yield
    tx.arrived(o0, reg(2, 0, 0), dev(1, 0))
    tx.arrived(o1, reg(2, 0, 1), dev(-1, 0))
    second[2] = ring(2, 0, 0, 1)
    yield
    opposite(0)
    yield
    along_q(-1)
    along_q(1)
    yield
    along_q(2)
    yield
    opposite(-1)
    opposite(1)
    yield
    opposite(2)
    yield


def split2(v):
    hi = v.astype(BF)
    return hi, (v - hi.astype(F32)).astype(BF)


def dot(a, b):
    return jnp.dot(a, b, preferred_element_type=F32)


def tables(meta):
    ex = lax.axis_index("expert").astype(F32)
    row = lax.broadcasted_iota(jnp.int32, (BLOCK, BLOCK), 0)
    col = lax.broadcasted_iota(jnp.int32, (BLOCK, BLOCK), 1)
    before = (row < col).astype(BF)
    quarter = lax.rem(lax.broadcasted_iota(jnp.int32, (GROUP, BLOCK), 0), 4).astype(F32)

    def one(ids, shares, which, cap):
        hit = (ids == which).astype(F32)
        named = jnp.sum(hit, axis=1)
        share = jnp.sum(hit * shares, axis=1)
        pos = dot(named.astype(BF), before) + quarter * cap
        return jnp.where(named > 0, pos, -1.0), share

    fid, pid, fsh, psh = (meta[:, 4 * i:4 * i + 4, :] for i in range(4))
    a = one(fid, fsh, 2.0 * ex, CAPF)
    b = one(fid, fsh, 2.0 * ex + 1.0, CAPF)
    p = one(pid, psh, ex, CAPP)
    return a, b, p


def quad_row(v, q):
    return jnp.concatenate([v[4 * q + i:4 * q + i + 1, :] for i in range(4)], axis=1)


def quad_col(v, first, q):
    return jnp.concatenate([v[:, first + 4 * q + i:first + 4 * q + i + 1] for i in range(4)], axis=0)


def pick(rows, pos):
    slot = lax.broadcasted_iota(jnp.int32, (rows, TOKQ), 0).astype(F32)
    return (slot == pos).astype(BF)


def put(rows, pos, share):
    slot = lax.broadcasted_iota(jnp.int32, (TOKQ, rows), 1).astype(F32)
    return jnp.where(slot == pos, share, 0.0)


COLS = WIDTH // NX
NEAR = ((0, 0), (1, 0), (-1, 0), (0, 1), (0, -1), (2, 0), (0, 2), (1, 1), (1, -1), (-1, 1), (-1, -1),
        (2, 1), (2, -1), (1, 2), (-1, 2), (2, 2))
CUTS = (0, 1, 3, 5, 9, 13, 16)
STEPS_P = ((0, 1), (1, 3), (3, 5), (5, 7), (7, 9), (9, 11), (11, 13), (13, 15), (15, 16))
PARTS = ((0, 5), (5, 9), (9, 13), (13, 16))
STRIPES = len(CUTS) - 1
ORDER = (4, 3, -3, 2, -2, 1, -1, 0)
SENDS = 6 * 20 + 2 * 17 + STRIPES * (8 + 14 + 17) + 2 * (GROUP - 1)

PLAN = (
    "umtmgutgmutmgutgmugmTugtutQQQgdQEguFguLlWPd0dP101P201212012d",
    "0dP1d2P301d3P2d1Pd403P434P2505145315043024V253504352452314C5",
    "334C54C5C",
)


def reduce_stripe(me, tx, cols, part, theirs, ring, out):
    half = BLOCK // 2

    def mine(k, h=None):
        at = slice(None) if h is None else pl.ds(h * half, half)
        return part.at[me.zz(k) * 2 + me.c, at, cols]

    def region(z, c, h):
        lo = (z * 2 + c) * BLOCK
        if h is None:
            return out.at[pl.ds(pl.multiple_of(lo, BLOCK), BLOCK), :]
        return out.at[pl.ds(pl.multiple_of(lo + h * half, half), half), :]

    swap = {k: tx.send(part.at[me.zz(k) * 2 + 1 - me.c, :, cols], theirs.at[me.zz(k)], me.partner()) for k in ORDER}
    yield

    def pair_sum(k):
        tx.arrived(swap[k], theirs.at[me.zz(k)], me.partner())
        r = mine(k)
        r[...] = (r[...].astype(F32) + theirs[me.zz(k)].astype(F32)).astype(BF)

    slot, waiting = {}, {}

    def push(sign, h, j):
        r = mine(sign * j, h)
        if (sign, h) in waiting:
            n, s = waiting[(sign, h)]
            tx.arrived(n, ring.at[s], me.dev_z(sign))
            r[...] = (r[...].astype(F32) + ring[s].astype(F32)).astype(BF)
        s = slot.setdefault((sign, h, j), len(slot))
        waiting[(sign, h)] = (tx.send(r, ring.at[s], me.dev_z(sign)), s)

    pair_sum(4)
    push(1, 0, 4)
    push(-1, 1, 4)
    pair_sum(3)
    pair_sum(-3)
    push(1, 1, 3)
    push(-1, 0, 3)
    yield
    for j in (3, 2, 1):
        if j < 3:
            pair_sum(j)
            pair_sum(-j)
            push(1, 1, j)
            push(-1, 0, j)
        push(1, 0, j)
        push(-1, 1, j)
        yield
    pair_sum(0)
    for h in (1, 0):
        total = mine(0, h)[...].astype(F32)
        for sign in (1, -1):
            n, s = waiting[(sign, h)]
            tx.arrived(n, ring.at[s], me.dev_z(sign))
            total = total + ring[s].astype(F32)
        region(me.z, me.c, h)[...] = total.astype(BF)
    yield from gather_z(me, tx, region(me.z, me.c, None), region)


def main_kernel(gate_i, up_i, down_i, tok_i, fid_i, pid_i, fsc_i, psc_i, first, second, ga_o, gb_o,
                big, down, tok, meta, x0, x1, acc, h0, h1, wt, low_s, low3, b3, rows, theirs, ring,
                sel, low_t, bt, hid_t, back, gbuf, gabuf, ra, rb, send_sem, recv_sem, loc_sem):
    me = Place()
    tx = Sender(send_sem, recv_sem)
    mine = pl.ds(pl.multiple_of(me.dp * BLOCK, BLOCK), BLOCK)
    loads = [
        pltpu.make_async_copy(s, d, loc_sem.at[i]) for i, (s, d) in enumerate((
            (tok_i, tok.at[me.ex]), (gate_i, big.at[0:2, mine, :]),
            (up_i, big.at[2:4, mine, :]), (down_i, down.at[:, :, 0:BLOCK])))
    ]
    for cp in loads:
        cp.start()
    fsc, psc = fsc_i[...], psc_i[...]
    meta[me.ex] = jnp.concatenate([
        fid_i[...].astype(F32), pid_i[...].astype(F32),
        fsc / jnp.sum(fsc, axis=0, keepdims=True), psc / jnp.sum(psc, axis=0, keepdims=True)], axis=0)
    barrier([me.dev_xy(*p) for p in NEAR[1:]] + [me.dev_z(1), me.dev_z(-1), me.partner()])

    def block_region(ref, size):
        def region(z, c, h):
            v = ref.at[z * 2 + c]
            return v if h is None else v.at[pl.ds(h * (size // 2), size // 2)]
        return region

    def rows_region(i):
        def region(dx, dy, h, ex, ey):
            dp = me.xy(dx, dy)
            if h is None:
                return big.at[i, pl.ds(pl.multiple_of(dp * BLOCK, BLOCK), BLOCK), :]
            n = BLOCK // 2
            return big.at[i, pl.ds(pl.multiple_of(dp * BLOCK + h * n, n), n), :]
        return region

    def cols_region(e):
        def region(dx, dy, h, ex, ey):
            j = [(a % NX, b % NX) for a, b in NEAR].index(((dx - ex) % NX, (dy - ey) % NX))
            rows_h = slice(None) if h is None else pl.ds(h * (HIDDEN // 2), HIDDEN // 2)
            return down.at[e, rows_h, j * BLOCK:(j + 1) * BLOCK]
        return region

    def own_half(ref, e):
        def half(h):
            v = ref.at[e]
            n = v.shape[0] // 2
            return v if h is None else v.at[pl.ds(h * n, n)]
        return half

    def stripe(r):
        return pl.ds(pl.multiple_of(lax.rem(me.y + r + NX, NX) * COLS, COLS), COLS)

    jobs = {
        "m": [gather_z(me, tx, meta.at[me.ex], block_region(meta, 16))],
        "t": [gather_z(me, tx, tok_i, block_region(tok, BLOCK))],
        "g": [gather_xy(me, tx, own_half(gate_i, e), rows_region(e), e == 0) for e in (0, 1)],
        "u": [gather_xy(me, tx, own_half(up_i, e), rows_region(2 + e), e == 0) for e in (0, 1)],
        "d": [gather_xy(me, tx, own_half(down_i, e), cols_region(e), e == 0) for e in (0, 1)],
    }
    def span(lo, hi):
        return slice(lo * BLOCK, hi * BLOCK)

    for i in range(STRIPES):
        lo, hi = CUTS[i], CUTS[i + 1]
        home = [k for k, (a, b) in enumerate(PARTS) if a <= lo < b][0]
        base = PARTS[home][0]
        jobs[str(i)] = [reduce_stripe(me, tx, span(lo, hi), tok, theirs.at[:, :, span(lo, hi)], ring.at[:, :, span(lo, hi)],
                                      big.at[home, :, span(lo - base, hi - base)])]

    kept = {}

    def table_step():
        for cp in loads:
            cp.wait()
        for j, off in enumerate(NEAR):
            bh, bl = split2(second[0, :, pl.ds(pl.multiple_of(me.xy(*off) * BLOCK, BLOCK), BLOCK)])
            b3[:, span(j, j + 1)] = jnp.concatenate([bh, bh, bl], axis=0)
        (pa, wa), (pb, wb), (pp, wp) = tables(meta[...])
        turned = jnp.transpose(jnp.concatenate([pa, pb, pp, -wa, -wb, wp, pp, wp], axis=0))
        for q in range(QUADS):
            wt[q] = jnp.concatenate([
                put(RF, quad_col(turned, 0, q), quad_col(turned, 48, q)),
                put(RP, quad_col(turned, 32, q), quad_col(turned, 80, q)),
                put(RF, quad_col(turned, 16, q), quad_col(turned, 64, q)),
            ], axis=1).astype(BF)
        kept["rows"] = (pa, pb, pp)
        kept["share"] = wp
        kept["quad"] = iter(range(QUADS))
        kept["part"] = iter(STEPS_P)
        kept["grad"] = iter(range(len(PARTS)))

    def gather_step():
        q = next(kept["quad"])
        pa, pb, pp = kept["rows"]
        oa, op, ob = pick(RF, quad_row(pa, q)), pick(RP, quad_row(pp, q)), pick(RF, quad_row(pb, q))
        sel[q] = op

        def body(i, _):
            at = pl.ds(pl.multiple_of(i * 512, 512), 512)
            t = tok[4 * q:4 * q + 4, :, at].reshape(TOKQ, 512)
            x0[q * RF:(q + 1) * RF, at] = dot(oa, t).astype(BF)
            x0[QUADS * RF + q * RP:QUADS * RF + (q + 1) * RP, at] = dot(op, t).astype(BF)
            x1[q * RF:(q + 1) * RF, at] = dot(ob, t).astype(BF)
            return 0

        lax.fori_loop(0, 4, body, 0)

    def product(x, e, m, first_row, parts, how, h=None):
        rows_m = x.shape[0] // m

        def body(i, _):
            lo = pl.multiple_of(lax.rem(i, m) * rows_m, rows_m)
            rr = pl.ds(lo, rows_m)
            ra_ = pl.ds(first_row + lo, rows_m)
            cc = pl.ds(pl.multiple_of(lax.div(i, m) * CHUNK, CHUNK), CHUNK)
            out = []
            for w in (0, 1):
                v = sum(dot(x[rr, stripe(r)], big[2 * w + e, stripe(r), cc]) for r in parts)
                out.append(v if how == "set" else acc[w, ra_, cc] + v)
            if how == "end":
                g, u = out
                h[rr, cc] = (g / (1.0 + jnp.exp(-g)) * u).astype(BF)
            else:
                acc[0, ra_, cc], acc[1, ra_, cc] = out
            return 0

        lax.fori_loop(0, m * (HIDDEN // CHUNK), body, 0)

    def row0_step():
        product(x0, 0, 2, 0, (0,), "set")
        product(x1, 1, 1, ROWS0, (0,), "set")

    def rows1_step():
        product(x0, 0, 2, 0, (-1, 1), "add")
        product(x1, 1, 1, ROWS0, (-1, 1), "add")

    def last0_step():
        product(x0, 0, 2, 0, (2,), "end", h0)

    def last1_step():
        product(x1, 1, 1, ROWS0, (2,), "end", h1)

    nt = (((1,), (1,)), ((), ()))
    tn = (((0,), (0,)), ((), ()))

    def low_step():
        tx.drain("mtgu")
        ah, al = split2(first[...])
        low2 = lax.dot_general(h0[QUADS * RF:, :], jnp.concatenate([ah, al], axis=0), nt, preferred_element_type=F32)
        low = low2[:, :RANK] + low2[:, RANK:]
        lh, ll = split2(low)
        low_s[...] = low
        low3[...] = jnp.concatenate([lh, ll, lh], axis=1)

    def spread_step():
        hid_t[...] = jnp.transpose(h0[QUADS * RF:, :])
        for q in range(QUADS):
            lq = low_s[q * RP:(q + 1) * RP, :]
            l1, l2 = split2(lq)
            l3 = (lq - l1.astype(F32) - l2.astype(F32)).astype(BF)
            s = lax.dot_general(jnp.concatenate([l1, l2, l3, jnp.zeros_like(l1)], axis=1), sel[q], tn,
                                preferred_element_type=F32)
            v = (s[0:RANK] + s[RANK:2 * RANK] + s[2 * RANK:3 * RANK]) * quad_row(kept["share"], q)
            hi, lo = split2(v)
            low_t[0:RANK, q * TOKQ:(q + 1) * TOKQ] = hi
            low_t[RANK:, q * TOKQ:(q + 1) * TOKQ] = lo

    def partial_step():
        at = span(*next(kept["part"]))
        n = at.stop - at.start
        r0 = dot(h0[...], down[0, :, at])
        rp = r0[QUADS * RF:] + dot(low3[...], b3[:, at])
        r1 = dot(h1[...], down[1, :, at])
        for q in range(QUADS):
            rows[q, 0:RF, 0:n] = r0[q * RF:(q + 1) * RF].astype(BF)
            rows[q, RF:RF + RP, 0:n] = rp[q * RP:(q + 1) * RP].astype(BF)
            rows[q, RF + RP:, 0:n] = r1[q * RF:(q + 1) * RF].astype(BF)
        for q in range(QUADS):
            tok[4 * q:4 * q + 4, :, at] = dot(wt[q], rows[q, :, 0:n]).astype(BF).reshape(4, BLOCK, n)

    got_b = {}

    def grad_b(i):
        lo, hi = PARTS[i]
        gb = dot(low_t[...], big[i, :, 0:(hi - lo) * BLOCK])
        gbuf[:, span(lo, hi)] = gb[:RANK] + gb[RANK:]
        tx.tag = "x"
        for j in reversed(range(max(lo, 1), hi)):
            got_b[j] = tx.send(gbuf.at[:, span(j, j + 1)], rb.at[j], me.dev_xy(*NEAR[j]))

    def grad_step():
        i = next(kept["grad"])
        lo, hi = PARTS[i]
        v = lax.dot_general(b3[RANK:, span(lo, hi)], big[i, :, 0:(hi - lo) * BLOCK], nt, preferred_element_type=F32)
        bt[...] = v if i == 0 else bt[...] + v
        if i < len(PARTS) - 1:
            grad_b(i)

    steps = {"T": table_step, "Q": gather_step, "E": row0_step, "F": rows1_step, "L": last0_step, "l": last1_step,
             "W": low_step, "V": spread_step, "P": partial_step, "C": grad_step}
    for op in "".join(PLAN):
        if op in steps:
            steps[op]()
        else:
            tx.tag = op
            for j in jobs[op]:
                next(j)

    na = HIDDEN // GROUP
    for q in range(QUADS):
        at = slice(q * TOKQ, (q + 1) * TOKQ)
        v = (bt[:RANK, at] + bt[RANK:, at]) * quad_row(kept["share"], q)
        hi, lo = split2(v)
        picked = lax.dot_general(sel[q], jnp.concatenate([hi, lo], axis=0), nt, preferred_element_type=F32)
        back[q * RP:(q + 1) * RP, :] = picked.astype(BF)
    ga = dot(hid_t[...], back[...])
    gabuf[...] = ga[:, :RANK] + ga[:, RANK:]
    tx.tag = "x"
    got_a = {}
    for j in reversed(range(1, GROUP)):
        lo = pl.multiple_of(me.xy(*NEAR[j]) * na, na)
        got_a[j] = tx.send(gabuf.at[pl.ds(lo, na)], ra.at[j], me.dev_xy(*NEAR[j]))
    grad_b(len(PARTS) - 1)
    tb = gbuf[:, 0:BLOCK]
    for j in range(1, GROUP):
        tx.arrived(got_b[j], rb.at[j], me.dev_xy(*NEAR[j]))
        tb = tb + rb[j]
    gb_o[...] = tb
    ta = gabuf[pl.ds(pl.multiple_of(me.dp * na, na), na), :]
    for j in range(1, GROUP):
        tx.arrived(got_a[j], ra.at[j], me.dev_xy(*NEAR[j]))
        ta = ta + ra[j]
    ga_o[...] = ta
    assert tx.count == SENDS
    tx.drain("mtgud012345x")


def main_call(gate, up, down, tok, fid, pid, fsc, psc, first, second):
    sds = jax.ShapeDtypeStruct
    vm = pltpu.VMEM
    na, nb = HIDDEN // GROUP, WIDTH // GROUP
    return pl.pallas_call(
        main_kernel,
        out_shape=(sds((na, RANK), F32), sds((RANK, nb), F32)),
        in_specs=[ANY] * 4 + [VM] * 6,
        out_specs=(VM, VM),
        scratch_shapes=[
            vm((4, WIDTH, HIDDEN), BF), vm((2, HIDDEN, WIDTH), BF),
            vm((GROUP, BLOCK, WIDTH), BF), vm((GROUP, 16, BLOCK), F32),
            vm((ROWS0, WIDTH), BF), vm((ROWS1, WIDTH), BF), vm((2, ROWS0 + ROWS1, HIDDEN), F32),
            vm((ROWS0, HIDDEN), BF), vm((ROWS1, HIDDEN), BF),
            vm((QUADS, TOKQ, RQ), BF), vm((QUADS * RP, RANK), F32), vm((QUADS * RP, 3 * RANK), BF),
            vm((3 * RANK, WIDTH), BF), vm((QUADS, RQ, CHUNK), BF),
            vm((NZ, BLOCK, WIDTH), BF), vm((14, BLOCK // 2, WIDTH), BF),
            vm((QUADS, RP, TOKQ), BF), vm((2 * RANK, GROUP * BLOCK), BF), vm((2 * RANK, GROUP * BLOCK), F32),
            vm((HIDDEN, QUADS * RP), BF), vm((QUADS * RP, 2 * RANK), BF), vm((RANK, WIDTH), F32),
            vm((HIDDEN, RANK), F32), vm((GROUP, na, RANK), F32), vm((GROUP, RANK, nb), F32),
            pltpu.SemaphoreType.DMA((SENDS,)), pltpu.SemaphoreType.DMA((SENDS,)), pltpu.SemaphoreType.DMA((4,)),
        ],
        compiler_params=pltpu.CompilerParams(collective_id=0, has_side_effects=True, vmem_limit_bytes=63 << 20),
        name="main",
    )(gate, up, down, tok, fid, pid, fsc, psc, first, second)


def shards(tokens, fid, pid, fsc, psc, gate, up, down, first, second):
    ga, gb = main_call(gate, up, down, tokens, fid.T, pid.T, fsc.T, psc.T, first[0].T, second)
    return ga[None], gb[None]


def solution(mesh):
    rows = P(("dp", "expert"), None)
    return jax.shard_map(
        shards,
        mesh=mesh,
        in_specs=(rows,) * 5 + (P("expert", "dp", None), P("expert", "dp", None), P("expert", None, "dp"),
                                P("expert", None, None), P("expert", None, None)),
        out_specs=(P("expert", "dp", None), P("expert", None, "dp")),
        check_vma=False,
    )
```
